32 devices in a mesh: dp: 2 (over y), expert: 16 (over z, x, core).
Axes of the slice: x: 2, y: 2, z: 4, core: 2. Of those that a mesh axis runs over, the one named last changes fastest.
Arguments:
- tokens: bfloat16 [512, 2880], P(('dp', 'expert')), may hold values from -6 to 6
- grad_out: bfloat16 [512, 2880], P(('dp', 'expert')), may hold values from -6 to 6
- route_ids: int32 [512, 4], P(('dp', 'expert')), may hold values from 0 to 4, all different within a row; in each aligned block of 16 rows (0 to 15, 16 to 31, ...) at most 16 rows name the same one
- route_prob: float32 [512, 4], P(('dp', 'expert')), may hold values from 0.05 to 1
- device_expert: int32 [16], replicated, may hold values from 0 to 4, as said below
- unit_count: int32 [16], replicated, may hold values from 264 to 480, as said below
- expert_weights: bfloat16 [16, 480, 8640], P('expert'), may hold values from -0.109375 to 0.109375
Outputs:
- grad_tokens: bfloat16 [512, 2880], P(('dp', 'expert'))
- grad_weights: bfloat16 [16, 480, 8640], P('expert', 'dp')
The draws below stay inside these ranges and needn't reach their ends.
Inputs may be any that keep to these rules, and one draw needn't show every extreme that they name: `route_ids`: each row names 4 different experts; the 16 rows of one device name each expert at most 16 times, and in every draw some device names some expert exactly 16 times. `device_expert`: aligned blocks of 16 indices of expert hold 5 experts, ids rising by one from 5 times the block's number; the indices of one expert are consecutive, 3 or 4 of them; every expert has a group. `unit_count`: the counts of the indices of one expert sum to 1440; rows of expert_weights at or past a slot's count are not part of the model.
All inputs are finite; a program needn't handle non-finite values.
Results may differ from the reference program's by a relative error of at most 0.0058.
Values may be sent and summed in bfloat16 or wider, within the bound.
A program may use at most 128 MiB of HBM per device.

```python
import math
import jax
import jax.numpy as jnp
import numpy as np
from jax import lax

D = 2880
HID = 1440
TOPK = 4
TOK_DEV = 16
SLOT = 480
EXPERTS = 5
CAP = 16
TOKENS = 512
N_DP = 2
N_EXPERT = 16


def plan_tables(key):
    blocks = N_EXPERT // 16
    larger = jax.random.randint(jax.random.fold_in(key, 11), (blocks,), 0, 5)
    group_sizes = 3 + (jnp.arange(5)[None, :] == larger[:, None]).astype(jnp.int32)
    group_ends = jnp.cumsum(group_sizes, axis=1)
    position = jnp.arange(16)
    local_id = jnp.sum((position[None, :, None] >= group_ends[:, None, :]).astype(jnp.int32), axis=2)
    experts = local_id + 5 * jnp.arange(blocks)[:, None]
    group_begin = jnp.take_along_axis(group_ends - group_sizes, local_id, axis=1)
    member = position[None, :] - group_begin
    group_size = jnp.take_along_axis(group_sizes, local_id, axis=1)
    unit_step = HID // 60
    shifts = jax.random.randint(jax.random.fold_in(key, 12), (blocks, 2), -4, 5) * unit_step
    shifts = shifts.at[0, 0].set(4 * unit_step)
    base_units = HID // 4
    parity_sign = 1 - 2 * (member % 2)
    pair_id = jnp.minimum(member // 2, 1)
    four_counts = base_units + parity_sign * jnp.take_along_axis(shifts, pair_id, axis=1)
    counts = jnp.where(group_size == 4, four_counts, HID // 3)
    return (experts.reshape(-1).astype(jnp.int32), counts.reshape(-1).astype(jnp.int32))


def draw_device_expert(key, part):
    return plan_tables(key)[0]


def draw_unit_count(key, part):
    return plan_tables(key)[1]


def block_levels(own_key, shape, pieces, low, largest):
    def one(axis_at, shards_of):
        draws = jax.random.uniform(jax.random.fold_in(jax.random.fold_in(own_key, 6), axis_at), (shards_of,), jnp.float32, low / len(pieces), largest / len(pieces))
        return jnp.repeat(jnp.exp(draws), shape[axis_at] // shards_of).reshape((-1,) + (1,) * (len(shape) - axis_at - 1))

    loudness = one(*pieces[0])
    for cut in pieces[1:]:
        loudness = loudness * one(*cut)
    return loudness


def routed_block(rng, own, number, rows, amount, top, limit, lean):
    order = jax.random.permutation(rng, amount)
    heavy_load, common = portions_of(amount, rows * top, limit, lean, True), portions_of(amount, rows * top, limit, lean, False)
    places = jnp.arange(amount)

    def named(tallies, rotation):
        used = int((tallies > 0).sum())
        fixed = max(1, used // 4)
        shifted = fixed + (places - fixed + rotation * (used - fixed)) % max(1, amount - fixed)
        return jnp.zeros((amount,), jnp.int32).at[order[jnp.where(places < fixed, places, shifted)]].set(jnp.asarray(tallies, jnp.int32))

    tallies = jnp.where(number % 4 == 0, named(heavy_load, number // 4), named(common, number - number // 4 - 1))
    mixed = jax.random.permutation(jax.random.fold_in(own, 3), amount)
    donor, taker = mixed[0:amount // 2 * 2:2], mixed[1:amount // 2 * 2:2]
    margin = jnp.minimum(tallies[donor] - 1, limit - tallies[taker]) // 2
    margin = jnp.where((donor == order[0]) | (taker == order[0]) | (tallies[taker] == 0), 0, jnp.maximum(margin, 0))
    shifted = jax.random.randint(jax.random.fold_in(own, 4), (amount // 2,), 0, 1 << 20) % (margin + 1)
    tallies = tallies.at[donor].add(-shifted).at[taker].add(shifted)
    labels = jnp.searchsorted(jnp.cumsum(tallies), jnp.arange(rows * top), side="right").astype(jnp.int32)
    grid = labels.reshape(top, rows).T
    grid = grid[jax.random.permutation(jax.random.fold_in(own, 1), rows)]
    rotation = jax.random.randint(jax.random.fold_in(own, 2), (rows, 1), 0, top)
    return jnp.take_along_axis(grid, (jnp.arange(top)[None, :] + rotation) % top, axis=1)


def portions_of(amount, total, most, skew, full):
    weights = [(1 << 20) // math.isqrt(rank ** skew) + 1 for rank in range(1, amount + 1)]
    largest = most if full else min(most, max(-(-total // amount), total * weights[0] // sum(weights)))
    least = 1 if total - largest >= amount - 1 else 0
    given, rest = [largest] + [least] * (amount - 1), total - largest - least * (amount - 1)
    while rest > 0:
        movable = [i for i in range(1, amount) if given[i] < largest] or [i for i in range(1, amount) if given[i] < most]
        whole, budget = sum([weights[i] for i in movable]), rest
        for i in movable:
            addition = min(most - given[i], max(1, budget * weights[i] // whole), rest)
            given[i] = given[i] + addition
            rest = rest - addition
    return np.array(given)


def bell_draw(rng, extent, deviation, bound, pieces=(), kind=jnp.bfloat16):
    values = deviation * jax.random.normal(rng, extent, jnp.float32)
    if pieces:
        values = values * block_levels(rng, extent, pieces, -0.22, 0.18)
    return jnp.clip(values, -bound, bound).astype(kind)


def setup_inputs(seed: int = 0) -> dict:
    keys = jax.random.split(jax.random.key(seed), 8)
    tokens = bell_draw(keys[0], (TOKENS, D), 1.0, 6.0, ((0, 32),))
    grad_out = bell_draw(keys[1], (TOKENS, D), 1.0, 6.0, ((0, 32),))
    route_ids_keys = jax.random.split(jax.random.fold_in(keys[2], 1), TOKENS // TOK_DEV)
    route_ids_turns = jax.random.permutation(jax.random.fold_in(keys[2], 3), TOKENS // TOK_DEV)
    route_ids = jax.vmap(lambda own, number: routed_block(jax.random.fold_in(keys[2], 2), own, number, TOK_DEV, EXPERTS, TOPK, CAP, 1))(route_ids_keys, route_ids_turns).reshape((TOKENS, TOPK))
    route_prob = jnp.clip(jnp.exp(math.log(1.0) - 2.9957323 * jax.random.uniform(keys[3], (TOKENS, TOPK), jnp.float32) ** block_levels(keys[3], (TOKENS, TOPK), ((0, 32),), -0.2, 0.2)), 0.05, 1.0)
    device_expert = draw_device_expert(jax.random.fold_in(keys[7], 71), 0)
    unit_count = draw_unit_count(jax.random.fold_in(keys[7], 71), 0)
    expert_weights = bell_draw(keys[6], (N_EXPERT, SLOT, 3 * D), D ** -0.5, 0.109375, ((0, 16),))
    return dict(tokens=tokens, grad_out=grad_out, route_ids=route_ids, route_prob=route_prob, device_expert=device_expert, unit_count=unit_count, expert_weights=expert_weights)


def silu_parts(preact):
    sigma = jax.nn.sigmoid(preact)
    return preact * sigma, sigma * (1.0 + preact * (1.0 - sigma))


def route_table(ids_block, prob_block):
    flat_ids = ids_block.reshape(-1)
    onehot = (flat_ids[:, None] == jnp.arange(EXPERTS, dtype=jnp.int32)[None, :]).astype(jnp.int32)
    rank_of = jnp.sum(onehot * jnp.cumsum(onehot, axis=0), axis=1) - 1
    matched = (flat_ids[None, None, :] == jnp.arange(EXPERTS, dtype=jnp.int32)[:, None, None]) & (rank_of[None, None, :] == jnp.arange(CAP, dtype=jnp.int32)[None, :, None])
    owner = jnp.arange(flat_ids.shape[0], dtype=jnp.int32) // TOPK
    token_ids = jnp.sum(jnp.where(matched, owner[None, None, :], 0), axis=2).astype(jnp.int32)
    route_weight = jnp.sum(jnp.where(matched, prob_block.reshape(-1)[None, None, :], 0.0), axis=2)
    live_slot = jnp.any(matched, axis=2)
    return token_ids, route_weight, live_slot


def reference(tokens, grad_out, route_ids, route_prob, device_expert, unit_count, expert_weights):
    sources = N_DP * N_EXPERT
    token_ids, route_weight, live_slot = jax.vmap(route_table)(route_ids.reshape(sources, TOK_DEV, TOPK), route_prob.reshape(sources, TOK_DEV, TOPK))
    token_ids = token_ids + (jnp.arange(sources, dtype=jnp.int32) * TOK_DEV)[:, None, None]
    contract = (((1,), (1,)), ((), ()))
    rows_first = (((0,), (0,)), ((), ()))

    def one_slot(accum, slot_index):
        expert_id = device_expert[slot_index]
        slot_weights = expert_weights[slot_index]
        row_index = jnp.take(token_ids, expert_id, axis=1).reshape(-1).astype(jnp.int32)
        row_scale = jnp.take(route_weight, expert_id, axis=1).reshape(-1)
        row_live = jnp.take(live_slot, expert_id, axis=1).reshape(-1)
        token_rows = jnp.where(row_live[:, None], tokens[row_index], jnp.zeros((), tokens.dtype))
        grad_rows = jnp.where(row_live[:, None], row_scale[:, None] * grad_out[row_index].astype(jnp.float32), 0.0).astype(jnp.bfloat16)
        gate_rows = slot_weights[:, :D]
        up_rows = slot_weights[:, D:2 * D]
        down_rows = slot_weights[:, 2 * D:]
        gate_pre = lax.dot_general(token_rows, gate_rows, contract, preferred_element_type=jnp.float32)
        up_pre = lax.dot_general(token_rows, up_rows, contract, preferred_element_type=jnp.float32)
        back_grad = lax.dot_general(grad_rows, down_rows, contract, preferred_element_type=jnp.float32)
        unit_mask = (jnp.arange(SLOT, dtype=jnp.int32) < unit_count[slot_index]).astype(jnp.float32)
        active, slope = silu_parts(gate_pre)
        hidden = (active * up_pre * unit_mask).astype(jnp.bfloat16)
        grad_gate = (back_grad * up_pre * slope * unit_mask).astype(jnp.bfloat16)
        grad_up = (back_grad * active * unit_mask).astype(jnp.bfloat16)
        partial_value = jnp.dot(grad_gate, gate_rows, preferred_element_type=jnp.float32) + jnp.dot(grad_up, up_rows, preferred_element_type=jnp.float32)
        accum = accum.at[row_index].add(jnp.where(row_live[:, None], partial_value, 0.0))
        grad_slot = jnp.concatenate([
            lax.dot_general(grad_gate, token_rows, rows_first, preferred_element_type=jnp.float32),
            lax.dot_general(grad_up, token_rows, rows_first, preferred_element_type=jnp.float32),
            lax.dot_general(hidden, grad_rows, rows_first, preferred_element_type=jnp.float32)], axis=1)
        return accum, grad_slot.astype(jnp.bfloat16)

    accum, grad_slots = lax.scan(one_slot, jnp.zeros((TOKENS, D), jnp.float32), jnp.arange(N_EXPERT, dtype=jnp.int32))
    return accum.astype(jnp.bfloat16), grad_slots
```

```python
import functools

import jax
import jax.numpy as jnp
from jax import lax
from jax.experimental import pallas as pl
from jax.experimental.pallas import tpu as pltpu
from jax.sharding import PartitionSpec as P

AXES = ("dp", "expert")


def silu_parts(preact):
    sigma = jax.nn.sigmoid(preact)
    return (preact * sigma, sigma * (1.0 + preact * (1.0 - sigma)))


def unit_work(token_rows, grad_rows, slot_weights, unit_mask):
    width = token_rows.shape[1]
    gate_rows = slot_weights[:, :width]
    up_rows = slot_weights[:, width : 2 * width]
    down_rows = slot_weights[:, 2 * width :]
    contract = (((1,), (1,)), ((), ()))
    gate_pre = lax.dot_general(token_rows, gate_rows, contract, preferred_element_type=jnp.float32)
    up_pre = lax.dot_general(token_rows, up_rows, contract, preferred_element_type=jnp.float32)
    back_grad = lax.dot_general(grad_rows, down_rows, contract, preferred_element_type=jnp.float32)
    active, slope = silu_parts(gate_pre)
    hidden = (active * up_pre * unit_mask).astype(jnp.bfloat16)
    grad_gate = (back_grad * up_pre * slope * unit_mask).astype(jnp.bfloat16)
    grad_up = (back_grad * active * unit_mask).astype(jnp.bfloat16)
    partial_value = jnp.dot(grad_gate, gate_rows, preferred_element_type=jnp.float32) + jnp.dot(
        grad_up, up_rows, preferred_element_type=jnp.float32
    )
    return (partial_value, hidden, grad_gate, grad_up)


def weight_terms(token_rows, grad_rows, hidden, grad_gate, grad_up):
    rows_first = (((0,), (0,)), ((), ()))
    return jnp.concatenate(
        [
            lax.dot_general(grad_gate, token_rows, rows_first, preferred_element_type=jnp.float32),
            lax.dot_general(grad_up, token_rows, rows_first, preferred_element_type=jnp.float32),
            lax.dot_general(hidden, grad_rows, rows_first, preferred_element_type=jnp.float32),
        ],
        axis=1,
    )


def send_back(partial_value):
    return lax.all_to_all(partial_value, "expert", split_axis=0, concat_axis=0, tiled=True)


def routed_shards(tokens, grad_out, route_ids, route_prob, device_expert, unit_count, expert_weights):
    token_count, width = tokens.shape
    top_count = route_ids.shape[1]
    devices = lax.axis_size("expert")
    experts = 5 * devices // 16
    capacity = token_count * top_count * 4 // devices
    flat_ids = route_ids.reshape(-1)
    onehot = (flat_ids[:, None] == jnp.arange(experts, dtype=jnp.int32)[None, :]).astype(jnp.int32)
    rank_of = jnp.sum(onehot * jnp.cumsum(onehot, axis=0), axis=1) - 1
    picked = (flat_ids[None, None, :] == device_expert[:, None, None]) & (
        rank_of[None, None, :] == jnp.arange(capacity, dtype=jnp.int32)[None, :, None]
    )
    picked = picked.astype(jnp.float32).reshape(devices * capacity, token_count * top_count)
    by_token = picked.reshape(devices * capacity, token_count, top_count).sum(axis=2)
    route_scale = jnp.dot(picked, route_prob.reshape(-1), precision=lax.Precision.HIGHEST)
    by_token_low = by_token.astype(jnp.bfloat16)
    sent_rows = jnp.dot(by_token_low, tokens, preferred_element_type=jnp.float32).astype(
        jnp.bfloat16
    )
    sent_grads = (
        route_scale[:, None] * jnp.dot(by_token_low, grad_out, preferred_element_type=jnp.float32)
    ).astype(jnp.bfloat16)
    outgoing = jnp.stack([sent_rows, sent_grads], axis=1).reshape(devices, capacity, 2, width)
    position = lax.axis_index("expert")
    unit_limit = lax.dynamic_index_in_dim(unit_count, position, keepdims=False)
    slot_weights = expert_weights[0]
    slot_units = slot_weights.shape[0]
    unit_mask = (jnp.arange(slot_units, dtype=jnp.int32) < unit_limit).astype(jnp.float32)
    arrived = lax.all_to_all(outgoing, "expert", split_axis=0, concat_axis=0, tiled=True)
    row_pairs = arrived.reshape(-1, 2, width)
    partial_value, hidden, grad_gate, grad_up = unit_work(
        row_pairs[:, 0], row_pairs[:, 1], slot_weights, unit_mask
    )
    leading = (arrived.shape[0], arrived.shape[1])
    returned, all_rows, hidden, grad_gate, grad_up = (
        send_back(partial_value.reshape(leading + (width,))),
        arrived,
        hidden.reshape(leading + (slot_units,)),
        grad_gate.reshape(leading + (slot_units,)),
        grad_up.reshape(leading + (slot_units,)),
    )
    row_pairs = all_rows.reshape(-1, 2, width)
    token_rows = row_pairs[:, 0]
    grad_rows = row_pairs[:, 1]
    hidden = hidden.reshape(-1, slot_units)
    grad_gate = grad_gate.reshape(-1, slot_units)
    grad_up = grad_up.reshape(-1, slot_units)
    term_block = weight_terms(token_rows, grad_rows, hidden, grad_gate, grad_up)
    grad_weights = lax.psum_scatter(term_block, "dp", scatter_dimension=0, tiled=True)
    parts = returned.reshape(devices * capacity, width)
    grad_tokens = lax.dot_general(
        by_token,
        parts,
        (((0,), (0,)), ((), ())),
        precision=lax.Precision.HIGHEST,
        preferred_element_type=jnp.float32,
    )
    return (grad_tokens.astype(jnp.bfloat16), grad_weights.astype(jnp.bfloat16)[None])


MESH = pl.DeviceIdType.MESH
STEP = 256
STRIPS = 4


def split_kernel(
    nz, half, tok, width, experts,
    x_in, g_in, w_in, ids_in, prob_in, expert_ref, limit_ref, gt_out, gw_out,
    xs, gs, own_g, ids, prob, w, wu, gate_pre, up_pre, acts, away_acts, acc,
    send1, recv1, send2, recv2, send3, recv3, gw,
    local_sem, recv_sem, sib_recv, sz, sx, sy, ss, act_send, act_recv, rs_send, rs_recv,
):
    f32, bf16 = jnp.float32, jnp.bfloat16
    y = lax.axis_index("dp")
    position = lax.axis_index("expert")
    z, x, c = position // 4, (position // 2) % 2, position % 2

    def place(yy, zz, xx, cc):
        return (yy, zz * 4 + xx * 2 + cc)

    zs = [lax.rem(z + k, nz) for k in range(nz)]
    x_nbr, y_nbr, sib = place(y, z, 1 - x, c), place(1 - y, z, x, c), place(y, z, x, 1 - c)
    z_nbrs = [place(y, zs[k], x, c) for k in range(1, nz)]
    z_sides = (place(y, lax.rem(z + nz - 1, nz), x, c), place(y, lax.rem(z + 1, nz), x, c))
    has_side = (z > 0, z < nz - 1)
    side_depth = (nz - 1 - z, z)
    barrier = pltpu.get_barrier_semaphore()
    peers = [x_nbr, y_nbr, sib] + z_nbrs
    for peer in peers:
        pl.semaphore_signal(barrier, inc=1, device_id=peer, device_id_type=MESH)

    line = nz * tok
    side_rows = 2 * line
    replica = 2 * side_rows

    def slot(ry, rc, rx, zz):
        return ((ry * 2 + rc) * 2 + rx) * nz + zz

    def rows(s, count=1):
        return pl.ds(pl.multiple_of(s * tok, tok), count * tok)

    mine = slot(0, 0, 0, z)
    own_x = pltpu.make_async_copy(x_in, xs.at[rows(mine)], local_sem.at[0])
    load_g = pltpu.make_async_copy(g_in, own_g, local_sem.at[1])
    load_ids = pltpu.make_async_copy(ids_in, ids, local_sem.at[2])
    load_prob = pltpu.make_async_copy(prob_in, prob, local_sem.at[3])
    for copy in (own_x, load_ids, load_prob, load_g):
        copy.start()
    load_w = []
    for h in range(2):
        first = pl.multiple_of((y if h == 0 else 1 - y) * half, 16)
        load_w.append(pltpu.make_async_copy(w_in.at[0, pl.ds(first, half)], w.at[h], local_sem.at[4 + h]))
        load_w[h].start()

    spare = gs.shape[1] - width
    lane = lax.broadcasted_iota(jnp.int32, (tok, spare), 1)
    diagonal = lax.broadcasted_iota(jnp.int32, (tok, tok), 0) == lax.broadcasted_iota(jnp.int32, (tok, tok), 1)

    def column(row):
        return jnp.sum(jnp.where(diagonal, jnp.broadcast_to(row, (tok, tok)), 0.0), axis=1, keepdims=True)

    load_ids.wait()
    load_prob.wait()
    scales = jnp.zeros((tok, spare), f32)
    which = (lane % experts).astype(f32)
    for k in range(ids.shape[0]):
        named = column(ids[k : k + 1, :].astype(f32))
        scales += jnp.where(named == which, column(prob[k : k + 1, :]), 0.0)
    high = scales.astype(bf16).astype(f32)
    middle = (scales - high).astype(bf16).astype(f32)
    term = lane // experts
    packed = jnp.where(term == 0, high, jnp.where(term == 1, middle, scales - high - middle))
    load_g.wait()
    gs[rows(mine), :width] = own_g[...]
    gs[rows(mine), width:] = jnp.where(term < 3, packed, 0.0).astype(bf16)
    own_x.wait()
    pl.semaphore_wait(barrier, len(peers))

    bufs = (xs, gs)

    def move(p, src, dst, target, send, recv, count=1):
        return pltpu.make_async_remote_copy(
            src_ref=bufs[p].at[rows(src, count)], dst_ref=bufs[p].at[rows(dst, count)],
            send_sem=send, recv_sem=recv, device_id=target, device_id_type=MESH,
        )

    def landing(p, ry, rx, zz):
        return recv_sem.at[p, (ry * 2 + rx) * nz + zz]

    def arrived(p, ry, rx, zz):
        s = slot(ry, 0, rx, zz)
        move(p, s, s, sib, ss.at[p, ry], landing(p, ry, rx, zz)).wait_recv()

    def z_send(p, ry, zz, side):
        s = slot(ry, 0, 0, zz)
        move(p, s, s, z_sides[side], sz.at[(p * 2 + ry) * 2 + side], landing(p, ry, 0, zz)).start()

    def x_send(p, zz):
        move(p, slot(0, 0, 0, zz), slot(0, 0, 1, zz), x_nbr, sx.at[p], landing(p, 0, 1, zz)).start()

    def y_send(p, rx, zz):
        move(p, slot(0, 0, rx, zz), slot(1, 0, rx, zz), y_nbr, sy.at[p], landing(p, 1, rx, zz)).start()

    def sib_send(p, ry, rx, zz):
        move(p, slot(ry, 0, rx, zz), slot(ry, 1, rx, zz), sib, ss.at[p, ry], sib_recv.at[p, ry]).start()

    def sib_arrived(p, ry):
        s = slot(ry, 1, 0, 0)
        move(p, s, s, sib, ss.at[p, ry], sib_recv.at[p, ry], 2 * nz).wait_recv()

    def at_distance(d, act):
        for side, zz in ((0, z - d), (1, z + d)):
            pl.when((zz >= 0) & (zz < nz))(functools.partial(act, side, zz))

    def from_z(side, zz):
        for p in range(2):
            arrived(p, 0, 0, zz)
            pl.when(has_side[1 - side])(lambda: z_send(p, 0, zz, 1 - side))
            x_send(p, zz)
            sib_send(p, 0, 0, zz)

    def relay_x(p, zz):
        arrived(p, 0, 1, zz)
        sib_send(p, 0, 1, zz)
        y_send(p, 1, zz)

    def cross_relay(side, zz):
        def go():
            for p in range(2):
                arrived(p, 1, 0, zz)
                z_send(p, 1, zz, 1 - side)
                sib_send(p, 1, 0, zz)
        pl.when(has_side[1 - side])(go)

    def cross_last(p, side, zz):
        def go():
            arrived(p, 1, 0, zz)
            sib_send(p, 1, 0, zz)
        pl.when(jnp.logical_not(has_side[1 - side]))(go)

    def cross_own(side):
        for p in range(2):
            z_send(p, 1, z, side)

    for p in range(2):
        for side in range(2):
            pl.when(has_side[side])(lambda: z_send(p, 0, z, side))
        x_send(p, z)
        y_send(p, 0, z)
        sib_send(p, 0, 0, z)
    late = nz - 2
    for d in range(1, nz):
        at_distance(d, from_z)
        if d == 1:
            for p in range(2):
                relay_x(p, z)
            for p in range(2):
                arrived(p, 1, 0, z)
                sib_send(p, 1, 0, z)
        elif d - 1 < late:
            for p in range(2):
                at_distance(d - 1, lambda side, zz: relay_x(p, zz))
        for side in range(2):
            ready = side_depth[side] <= 1 if d == 1 else side_depth[side] == d
            pl.when(has_side[side] & ready)(lambda: cross_own(side))

    expert = expert_ref[position]
    lane = lax.broadcasted_iota(jnp.int32, (1, 128), 1) - (128 - spare)
    sel = jnp.where((lane >= 0) & (lane < 3 * experts) & (lane % experts == expert), 1.0, 0.0)
    contract = (((1,), (1,)), ((), ()))
    tail = width // 128 * 128

    for h in range(2):
        load_w[h].wait()
        wu[h] = w[h, :, width : 2 * width]
    at_distance(1, cross_relay)
    for d in range(late, nz):
        at_distance(d, lambda side, zz: relay_x(0, zz))
    sib_arrived(0, 0)
    for h in range(2):
        gate_pre[h] = lax.dot_general(xs[:replica, :], w[h, :, :width], contract, preferred_element_type=f32)
    for d in range(late, nz):
        at_distance(d, lambda side, zz: relay_x(1, zz))
    for d in range(2, nz - 1):
        at_distance(d, cross_relay)
    for h in range(2):
        up_pre[h] = lax.dot_general(xs[:replica, :], wu[h], contract, preferred_element_type=f32)
    sib_arrived(1, 0)

    act_sends = [
        pltpu.make_async_remote_copy(
            src_ref=away_acts.at[k], dst_ref=acts.at[k, pl.ds(replica, replica)],
            send_sem=act_send.at[k], recv_sem=act_recv.at[k], device_id=y_nbr, device_id_type=MESH,
        )
        for k in range(3)
    ]
    scale = jnp.sum(gs[:replica, tail:].astype(f32) * sel, axis=1, keepdims=True)
    for h in (1, 0):
        b = scale * lax.dot_general(
            gs[:replica, :width], w[h, :, 2 * width :], contract, preferred_element_type=f32
        )
        unit = lax.broadcasted_iota(jnp.int32, (1, half), 1) + (y if h == 0 else 1 - y) * half
        unit_mask = jnp.where(unit < limit_ref[position], 1.0, 0.0)
        g, v = gate_pre[h], up_pre[h]
        live = jnp.broadcast_to(unit_mask, g.shape) > 0.0
        sigma = 1.0 / (1.0 + jnp.exp(-g))
        active = g * sigma
        gg = jnp.where(live, b * v * (sigma * (1.0 + g * (1.0 - sigma))), 0.0).astype(bf16)
        gu = jnp.where(live, b * active, 0.0).astype(bf16)
        hid = jnp.where(live, active * v * scale, 0.0).astype(bf16)
        for k, value in enumerate((gg, gu, hid)):
            if h == 0:
                acts[k, :replica, :] = value
            else:
                away_acts[k] = value
                act_sends[k].start()

    quarter = (width // 128 + STRIPS) // STRIPS * 128
    strips = [(at, min(at + quarter, width)) for at in range(0, width, quarter)]
    count = len(strips)

    def spans(begin, end):
        return [(at, min(STEP, end - at)) for at in range(begin, end, STEP)]

    def exchange(stage, i, src, dst, target):
        return pltpu.make_async_remote_copy(
            src_ref=src, dst_ref=dst, send_sem=rs_send.at[stage * count + i],
            recv_sem=rs_recv.at[stage * count + i], device_id=target, device_id_type=MESH,
        )

    def cols(i):
        begin, end = strips[i]
        return pl.ds(begin, end - begin)

    core = [exchange(0, i, send1.at[:, cols(i)], recv1.at[:, cols(i)], sib) for i in range(count)]
    second = [exchange(1, i, send2.at[:, cols(i)], recv2.at[:, cols(i)], x_nbr) for i in range(count)]
    third = [
        exchange(2, i, send3.at[pl.ds(0, (nz - 1) * tok), cols(i)], recv3.at[:, cols(i)], z_nbrs[0])
        for i in range(count)
    ]

    def first_stage(i):
        for at, size in spans(*strips[i]):
            span = slice(at, at + size)
            value = jnp.dot(acts[0, :replica, :], w[0, :, span], preferred_element_type=f32)
            value += jnp.dot(acts[1, :replica, :], wu[0, :, span], preferred_element_type=f32)
            value += jnp.dot(away_acts[0], w[1, :, span], preferred_element_type=f32)
            value += jnp.dot(away_acts[1], wu[1, :, span], preferred_element_type=f32)
            send1[:, span] = value[side_rows:].astype(bf16)
            acc[:, span] = value[:side_rows]
        core[i].start()

    def second_stage(i):
        span = slice(*strips[i])
        core[i].wait()
        send2[:, span] = (acc[line:, span] + recv1[line:, span].astype(f32)).astype(bf16)
        second[i].start()
        acc[:line, span] = acc[:line, span] + recv1[:line, span].astype(f32)

    def third_stage(i):
        span = slice(*strips[i])
        second[i].wait()
        value = acc[:line, span] + recv2[:, span].astype(f32)
        send3[:, span] = value.astype(bf16)
        for k in range(1, nz):
            exchange(
                2, i, send3.at[rows(zs[k]), cols(i)], recv3.at[pl.ds((k - 1) * tok, tok), cols(i)], z_nbrs[k - 1]
            ).start()
        acc[:line, span] = value

    def last_stage(i):
        span = slice(*strips[i])
        third[i].wait()
        total = acc[rows(z), span]
        for k in range(1, nz):
            total = total + recv3[(k - 1) * tok : k * tok, span].astype(f32)
        gt_out[:, span] = total.astype(bf16)

    def weight_term(k, right):
        turned = acts[k].T
        for at, size in spans(0, width):
            value = jnp.dot(turned, right[:, at : at + size], preferred_element_type=f32)
            gw[:, k * width + at : k * width + at + size] = value.astype(bf16)

    for i in range(count):
        first_stage(i)
        if i > 0:
            second_stage(i - 1)
    second_stage(count - 1)
    for p in range(2):
        for d in range(1, nz):
            at_distance(d, functools.partial(cross_last, p))
        for zz in range(nz):
            arrived(p, 1, 1, zz)
            sib_send(p, 1, 1, zz)

    def terms(k):
        if k < 2:
            if k == 0:
                sib_arrived(0, 1)
            act_sends[k].wait_recv()
            weight_term(k, xs)
        elif k == 2:
            sib_arrived(1, 1)
            act_sends[k].wait_recv()
            weight_term(k, gs)

    for i in range(count):
        third_stage(i)
        terms(i)
    for k in range(count, 3):
        terms(k)
    store_w = pltpu.make_async_copy(gw, gw_out.at[0], local_sem.at[6])
    store_w.start()

    def sent(p, ry, side, chunks):
        s = slot(ry, 0, 0, 0)
        move(p, s, s, z_sides[side], sz.at[(p * 2 + ry) * 2 + side], landing(p, ry, 0, 0), chunks).wait_send()

    for p in range(2):
        for ry in range(2):
            for side in range(2):
                for depth in range(nz - 1):
                    pl.when(side_depth[side] == depth)(lambda: sent(p, ry, side, depth + 1))
            move(p, 0, 0, sib, ss.at[p, ry], sib_recv.at[p, ry], 2 * nz).wait_send()
        move(p, 0, 0, x_nbr, sx.at[p], landing(p, 0, 1, 0), nz).wait_send()
        move(p, 0, 0, y_nbr, sy.at[p], landing(p, 1, 0, 0), nz + 1).wait_send()
    for copy in act_sends:
        copy.wait_send()
    for i in range(count):
        last_stage(i)
    store_w.wait()


def dense_shards(tokens, grad_out, route_ids, route_prob, device_expert, unit_count, expert_weights):
    tok, width = tokens.shape
    devices = lax.axis_size("expert")
    nz = devices // 4
    experts = 5 * devices // 16
    half = expert_weights.shape[1] // lax.axis_size("dp")
    spare = 128 - width % 128
    assert 3 * experts <= spare
    padded = width + spare
    replica = devices * tok
    line = nz * tok
    top = route_ids.shape[1]
    bf16, f32 = jnp.bfloat16, jnp.float32
    vmem = pltpu.VMEM
    dma = pltpu.SemaphoreType.DMA
    any_spec = pl.BlockSpec(memory_space=pl.ANY)
    smem_spec = pl.BlockSpec(memory_space=pltpu.SMEM)
    vmem_spec = pl.BlockSpec(memory_space=pltpu.VMEM)
    return pl.pallas_call(
        functools.partial(split_kernel, nz, half, tok, width, experts),
        out_shape=(
            jax.ShapeDtypeStruct((tok, width), bf16),
            jax.ShapeDtypeStruct((1, half, 3 * width), bf16),
        ),
        in_specs=[any_spec] * 5 + [smem_spec] * 2,
        out_specs=(vmem_spec, any_spec),
        scratch_shapes=[
            vmem((2 * replica, width), bf16), vmem((2 * replica, padded), bf16), vmem((tok, width), bf16),
            vmem((top, tok), jnp.int32), vmem((top, tok), f32),
            vmem((2, half, 3 * width), bf16), vmem((2, half, width), bf16),
            vmem((2, replica, half), f32), vmem((2, replica, half), f32),
            vmem((3, 2 * replica, half), bf16), vmem((3, replica, half), bf16),
            vmem((2 * line, width), f32),
            vmem((2 * line, width), bf16), vmem((2 * line, width), bf16),
            vmem((line, width), bf16), vmem((line, width), bf16),
            vmem((line, width), bf16), vmem(((nz - 1) * tok, width), bf16),
            vmem((half, 3 * width), bf16),
            dma((7,)), dma((2, 4 * nz)), dma((2, 2)), dma((8,)), dma((2,)), dma((2,)), dma((2, 2)),
            dma((3,)), dma((3,)), dma((3 * STRIPS,)), dma((3 * STRIPS,)),
        ],
        compiler_params=pltpu.CompilerParams(
            collective_id=0, has_side_effects=True, vmem_limit_bytes=60 * 1024 * 1024
        ),
        name="split_backward",
    )(tokens, grad_out, expert_weights, route_ids.T, route_prob.T, device_expert, unit_count)


def shards(tokens, grad_out, route_ids, *rest):
    token_count = tokens.shape[0]
    capacity = token_count * route_ids.shape[1] * 4 // lax.axis_size("expert")
    form = dense_shards if capacity >= token_count else routed_shards
    return form(tokens, grad_out, route_ids, *rest)


def solution(mesh):
    in_specs = (P(AXES, None),) * 4 + (P(), P(), P("expert", None, None))
    out_specs = (P(AXES, None), P("expert", "dp", None))
    return jax.shard_map(shards, mesh=mesh, in_specs=in_specs, out_specs=out_specs, check_vma=False)
```

```python
import functools

import jax
import jax.numpy as jnp
from jax import lax
from jax.experimental import pallas as pl
from jax.experimental.pallas import tpu as pltpu
from jax.sharding import PartitionSpec as P

AXES = ("dp", "expert")


def silu_parts(preact):
    sigma = jax.nn.sigmoid(preact)
    return (preact * sigma, sigma * (1.0 + preact * (1.0 - sigma)))


def unit_work(token_rows, grad_rows, slot_weights, unit_mask):
    width = token_rows.shape[1]
    gate_rows = slot_weights[:, :width]
    up_rows = slot_weights[:, width : 2 * width]
    down_rows = slot_weights[:, 2 * width :]
    contract = (((1,), (1,)), ((), ()))
    gate_pre = lax.dot_general(token_rows, gate_rows, contract, preferred_element_type=jnp.float32)
    up_pre = lax.dot_general(token_rows, up_rows, contract, preferred_element_type=jnp.float32)
    back_grad = lax.dot_general(grad_rows, down_rows, contract, preferred_element_type=jnp.float32)
    active, slope = silu_parts(gate_pre)
    hidden = (active * up_pre * unit_mask).astype(jnp.bfloat16)
    grad_gate = (back_grad * up_pre * slope * unit_mask).astype(jnp.bfloat16)
    grad_up = (back_grad * active * unit_mask).astype(jnp.bfloat16)
    partial_value = jnp.dot(grad_gate, gate_rows, preferred_element_type=jnp.float32) + jnp.dot(
        grad_up, up_rows, preferred_element_type=jnp.float32
    )
    return (partial_value, hidden, grad_gate, grad_up)


def weight_terms(token_rows, grad_rows, hidden, grad_gate, grad_up):
    rows_first = (((0,), (0,)), ((), ()))
    return jnp.concatenate(
        [
            lax.dot_general(grad_gate, token_rows, rows_first, preferred_element_type=jnp.float32),
            lax.dot_general(grad_up, token_rows, rows_first, preferred_element_type=jnp.float32),
            lax.dot_general(hidden, grad_rows, rows_first, preferred_element_type=jnp.float32),
        ],
        axis=1,
    )


def send_back(partial_value):
    return lax.all_to_all(partial_value, "expert", split_axis=0, concat_axis=0, tiled=True)


def routed_shards(tokens, grad_out, route_ids, route_prob, device_expert, unit_count, expert_weights):
    token_count, width = tokens.shape
    top_count = route_ids.shape[1]
    devices = lax.axis_size("expert")
    experts = 5 * devices // 16
    capacity = token_count * top_count * 4 // devices
    flat_ids = route_ids.reshape(-1)
    onehot = (flat_ids[:, None] == jnp.arange(experts, dtype=jnp.int32)[None, :]).astype(jnp.int32)
    rank_of = jnp.sum(onehot * jnp.cumsum(onehot, axis=0), axis=1) - 1
    picked = (flat_ids[None, None, :] == device_expert[:, None, None]) & (
        rank_of[None, None, :] == jnp.arange(capacity, dtype=jnp.int32)[None, :, None]
    )
    picked = picked.astype(jnp.float32).reshape(devices * capacity, token_count * top_count)
    by_token = picked.reshape(devices * capacity, token_count, top_count).sum(axis=2)
    route_scale = jnp.dot(picked, route_prob.reshape(-1), precision=lax.Precision.HIGHEST)
    by_token_low = by_token.astype(jnp.bfloat16)
    sent_rows = jnp.dot(by_token_low, tokens, preferred_element_type=jnp.float32).astype(
        jnp.bfloat16
    )
    sent_grads = (
        route_scale[:, None] * jnp.dot(by_token_low, grad_out, preferred_element_type=jnp.float32)
    ).astype(jnp.bfloat16)
    outgoing = jnp.stack([sent_rows, sent_grads], axis=1).reshape(devices, capacity, 2, width)
    position = lax.axis_index("expert")
    unit_limit = lax.dynamic_index_in_dim(unit_count, position, keepdims=False)
    slot_weights = expert_weights[0]
    slot_units = slot_weights.shape[0]
    unit_mask = (jnp.arange(slot_units, dtype=jnp.int32) < unit_limit).astype(jnp.float32)
    arrived = lax.all_to_all(outgoing, "expert", split_axis=0, concat_axis=0, tiled=True)
    row_pairs = arrived.reshape(-1, 2, width)
    partial_value, hidden, grad_gate, grad_up = unit_work(
        row_pairs[:, 0], row_pairs[:, 1], slot_weights, unit_mask
    )
    leading = (arrived.shape[0], arrived.shape[1])
    returned, all_rows, hidden, grad_gate, grad_up = (
        send_back(partial_value.reshape(leading + (width,))),
        arrived,
        hidden.reshape(leading + (slot_units,)),
        grad_gate.reshape(leading + (slot_units,)),
        grad_up.reshape(leading + (slot_units,)),
    )
    row_pairs = all_rows.reshape(-1, 2, width)
    token_rows = row_pairs[:, 0]
    grad_rows = row_pairs[:, 1]
    hidden = hidden.reshape(-1, slot_units)
    grad_gate = grad_gate.reshape(-1, slot_units)
    grad_up = grad_up.reshape(-1, slot_units)
    term_block = weight_terms(token_rows, grad_rows, hidden, grad_gate, grad_up)
    grad_weights = lax.psum_scatter(term_block, "dp", scatter_dimension=0, tiled=True)
    parts = returned.reshape(devices * capacity, width)
    grad_tokens = lax.dot_general(
        by_token,
        parts,
        (((0,), (0,)), ((), ())),
        precision=lax.Precision.HIGHEST,
        preferred_element_type=jnp.float32,
    )
    return (grad_tokens.astype(jnp.bfloat16), grad_weights.astype(jnp.bfloat16)[None])


MESH = pl.DeviceIdType.MESH
STEP = 256
STRIPS = 4
VMEM_BYTES = 67043328


def split_kernel(
    nz, half, tok, width, experts,
    x_in, g_in, w_in, ids_in, prob_in, expert_ref, limit_ref, gt_out, gw,
    xs, gs, own_g, ids, prob, w, wu, gate_pre, up_pre, acts, away_acts, acc,
    send1, recv1, send2, recv2, send3, recv3,
    local_sem, recv_sem, sib_recv, sz, sx, sy, ss, rs_send, rs_recv,
):
    f32, bf16 = jnp.float32, jnp.bfloat16
    y = lax.axis_index("dp")
    position = lax.axis_index("expert")
    z, x, c = position // 4, (position // 2) % 2, position % 2

    def place(yy, zz, xx, cc):
        return (yy, zz * 4 + xx * 2 + cc)

    zs = [lax.rem(z + k, nz) for k in range(nz)]
    x_nbr, y_nbr, sib = place(y, z, 1 - x, c), place(1 - y, z, x, c), place(y, z, x, 1 - c)
    z_nbrs = [place(y, zs[k], x, c) for k in range(1, nz)]
    z_sides = (place(y, lax.rem(z + nz - 1, nz), x, c), place(y, lax.rem(z + 1, nz), x, c))
    has_side = (z > 0, z < nz - 1)
    side_depth = (nz - 1 - z, z)
    barrier = pltpu.get_barrier_semaphore()
    peers = [x_nbr, y_nbr, sib] + z_nbrs
    for peer in peers:
        pl.semaphore_signal(barrier, inc=1, device_id=peer, device_id_type=MESH)

    line = nz * tok
    side_rows = 2 * line
    replica = 2 * side_rows

    def slot(ry, rc, rx, zz):
        return ((ry * 2 + rc) * 2 + rx) * nz + zz

    def rows(s, count=1):
        return pl.ds(pl.multiple_of(s * tok, tok), count * tok)

    mine = slot(0, 0, 0, z)
    own_x = pltpu.make_async_copy(x_in, xs.at[rows(mine)], local_sem.at[0])
    load_g = pltpu.make_async_copy(g_in, own_g, local_sem.at[1])
    load_ids = pltpu.make_async_copy(ids_in, ids, local_sem.at[2])
    load_prob = pltpu.make_async_copy(prob_in, prob, local_sem.at[3])
    for copy in (own_x, load_ids, load_prob, load_g):
        copy.start()
    load_w = []
    for h in range(2):
        first = pl.multiple_of((y if h == 0 else 1 - y) * half, 16)
        load_w.append(pltpu.make_async_copy(w_in.at[0, pl.ds(first, half)], w.at[h], local_sem.at[4 + h]))
        load_w[h].start()

    spare = gs.shape[1] - width
    lane = lax.broadcasted_iota(jnp.int32, (tok, spare), 1)
    diagonal = lax.broadcasted_iota(jnp.int32, (tok, tok), 0) == lax.broadcasted_iota(jnp.int32, (tok, tok), 1)

    def column(row):
        return jnp.sum(jnp.where(diagonal, jnp.broadcast_to(row, (tok, tok)), 0.0), axis=1, keepdims=True)

    load_ids.wait()
    load_prob.wait()
    scales = jnp.zeros((tok, spare), f32)
    which = (lane % experts).astype(f32)
    for k in range(ids.shape[0]):
        named = column(ids[k : k + 1, :].astype(f32))
        scales += jnp.where(named == which, column(prob[k : k + 1, :]), 0.0)
    high = scales.astype(bf16).astype(f32)
    middle = (scales - high).astype(bf16).astype(f32)
    term = lane // experts
    packed = jnp.where(term == 0, high, jnp.where(term == 1, middle, scales - high - middle))
    load_g.wait()
    gs[rows(mine), :width] = own_g[...]
    gs[rows(mine), width:] = jnp.where(term < 3, packed, 0.0).astype(bf16)
    own_x.wait()
    pl.semaphore_wait(barrier, len(peers))

    bufs = (xs, gs)

    def move(p, src, dst, target, send, recv, count=1):
        return pltpu.make_async_remote_copy(
            src_ref=bufs[p].at[rows(src, count)], dst_ref=bufs[p].at[rows(dst, count)],
            send_sem=send, recv_sem=recv, device_id=target, device_id_type=MESH,
        )

    def landing(p, ry, rx, zz):
        return recv_sem.at[p, (ry * 2 + rx) * nz + zz]

    def arrived(p, ry, rx, zz):
        s = slot(ry, 0, rx, zz)
        move(p, s, s, sib, ss.at[p, ry], landing(p, ry, rx, zz)).wait_recv()

    def z_send(p, ry, zz, side):
        s = slot(ry, 0, 0, zz)
        move(p, s, s, z_sides[side], sz.at[(p * 2 + ry) * 2 + side], landing(p, ry, 0, zz)).start()

    def x_send(p, zz):
        move(p, slot(0, 0, 0, zz), slot(0, 0, 1, zz), x_nbr, sx.at[p], landing(p, 0, 1, zz)).start()

    def y_send(p, rx, zz):
        move(p, slot(0, 0, rx, zz), slot(1, 0, rx, zz), y_nbr, sy.at[p], landing(p, 1, rx, zz)).start()

    def sib_send(p, ry, rx, zz):
        move(p, slot(ry, 0, rx, zz), slot(ry, 1, rx, zz), sib, ss.at[p, ry], sib_recv.at[p, ry]).start()

    def sib_arrived(p, ry):
        s = slot(ry, 1, 0, 0)
        move(p, s, s, sib, ss.at[p, ry], sib_recv.at[p, ry], 2 * nz).wait_recv()

    def at_distance(d, act):
        for side, zz in ((0, z - d), (1, z + d)):
            pl.when((zz >= 0) & (zz < nz))(functools.partial(act, side, zz))

    def from_z(side, zz):
        for p in range(2):
            arrived(p, 0, 0, zz)
            pl.when(has_side[1 - side])(lambda: z_send(p, 0, zz, 1 - side))
            x_send(p, zz)
            if p == 1:
                y_send(1, 0, zz)
            sib_send(p, 0, 0, zz)

    def relay_x(p, zz):
        arrived(p, 0, 1, zz)
        sib_send(p, 0, 1, zz)
        y_send(p, 1, zz)

    def cross_relay(side, zz):
        def go():
            arrived(0, 1, 0, zz)
            z_send(0, 1, zz, 1 - side)
            sib_send(0, 1, 0, zz)
        pl.when(has_side[1 - side])(go)

    def cross_last(side, zz):
        def go():
            arrived(0, 1, 0, zz)
            sib_send(0, 1, 0, zz)
        pl.when(jnp.logical_not(has_side[1 - side]))(go)

    for p in range(2):
        for side in range(2):
            pl.when(has_side[side])(lambda: z_send(p, 0, z, side))
        x_send(p, z)
        y_send(p, 0, z)
        sib_send(p, 0, 0, z)
    late = nz - 2
    for d in range(1, nz):
        at_distance(d, from_z)
        if d == 1:
            for p in range(2):
                relay_x(p, z)
            arrived(0, 1, 0, z)
            sib_send(0, 1, 0, z)
        elif d - 1 < late:
            for p in range(2):
                at_distance(d - 1, lambda side, zz: relay_x(p, zz))
        for side in range(2):
            ready = side_depth[side] <= 1 if d == 1 else side_depth[side] == d
            pl.when(has_side[side] & ready)(lambda: z_send(0, 1, z, side))

    expert = expert_ref[position]
    lane = lax.broadcasted_iota(jnp.int32, (1, 128), 1) - (128 - spare)
    sel = jnp.where((lane >= 0) & (lane < 3 * experts) & (lane % experts == expert), 1.0, 0.0)
    contract = (((1,), (1,)), ((), ()))
    tail = width // 128 * 128

    for h in range(2):
        load_w[h].wait()
        wu[h] = w[h, :, width : 2 * width]
    at_distance(1, cross_relay)
    for d in range(late, nz):
        at_distance(d, lambda side, zz: relay_x(0, zz))
    sib_arrived(0, 0)
    for h in range(2):
        gate_pre[h] = lax.dot_general(xs[:replica, :], w[h, :, :width], contract, preferred_element_type=f32)
    for d in range(late, nz):
        at_distance(d, lambda side, zz: relay_x(1, zz))
    for d in range(2, nz - 1):
        at_distance(d, cross_relay)
    for h in range(2):
        up_pre[h] = lax.dot_general(xs[:replica, :], wu[h], contract, preferred_element_type=f32)
    sib_arrived(1, 0)

    def activate(h, ry, gate, up):
        r = slice(ry * replica, (ry + 1) * replica)
        scale = jnp.sum(gs[r, tail:].astype(f32) * sel, axis=1, keepdims=True)
        b = scale * lax.dot_general(gs[r, :width], w[h, :, 2 * width :], contract, preferred_element_type=f32)
        unit = lax.broadcasted_iota(jnp.int32, (1, half), 1) + (y if h == 0 else 1 - y) * half
        unit_mask = jnp.where(unit < limit_ref[position], 1.0, 0.0)
        g, v = gate[...], up[...]
        live = jnp.broadcast_to(unit_mask, g.shape) > 0.0
        sigma = 1.0 / (1.0 + jnp.exp(-g))
        active = g * sigma
        gg = jnp.where(live, b * v * (sigma * (1.0 + g * (1.0 - sigma))), 0.0).astype(bf16)
        gu = jnp.where(live, b * active, 0.0).astype(bf16)
        if h == 0:
            acts[0, r, :] = gg
            acts[1, r, :] = gu
            acts[2, r, :] = jnp.where(live, active * v * scale, 0.0).astype(bf16)
        else:
            away_acts[0] = gg
            away_acts[1] = gu

    for h in range(2):
        activate(h, 0, gate_pre.at[h], up_pre.at[h])

    quarter = (width // 128 + STRIPS) // STRIPS * 128
    strips = [(at, min(at + quarter, width)) for at in range(0, width, quarter)]
    count = len(strips)

    def spans(begin, end):
        return [(at, min(STEP, end - at)) for at in range(begin, end, STEP)]

    def exchange(stage, i, src, dst, target):
        return pltpu.make_async_remote_copy(
            src_ref=src, dst_ref=dst, send_sem=rs_send.at[stage * count + i],
            recv_sem=rs_recv.at[stage * count + i], device_id=target, device_id_type=MESH,
        )

    def cols(i):
        begin, end = strips[i]
        return pl.ds(begin, end - begin)

    core = [exchange(0, i, send1.at[:, cols(i)], recv1.at[:, cols(i)], sib) for i in range(count)]
    second = [exchange(1, i, send2.at[:, cols(i)], recv2.at[:, cols(i)], x_nbr) for i in range(count)]
    third = [
        exchange(2, i, send3.at[pl.ds(0, (nz - 1) * tok), cols(i)], recv3.at[:, cols(i)], z_nbrs[0])
        for i in range(count)
    ]

    def first_stage(i):
        for at, size in spans(*strips[i]):
            span = slice(at, at + size)
            value = jnp.dot(acts[0, :replica, :], w[0, :, span], preferred_element_type=f32)
            value += jnp.dot(acts[1, :replica, :], wu[0, :, span], preferred_element_type=f32)
            value += jnp.dot(away_acts[0], w[1, :, span], preferred_element_type=f32)
            value += jnp.dot(away_acts[1], wu[1, :, span], preferred_element_type=f32)
            send1[:, span] = value[side_rows:].astype(bf16)
            acc[:, span] = value[:side_rows]
        core[i].start()

    def second_stage(i):
        span = slice(*strips[i])
        core[i].wait()
        send2[:, span] = (acc[line:, span] + recv1[line:, span].astype(f32)).astype(bf16)
        second[i].start()
        acc[:line, span] = acc[:line, span] + recv1[:line, span].astype(f32)

    def third_stage(i):
        span = slice(*strips[i])
        second[i].wait()
        value = acc[:line, span] + recv2[:, span].astype(f32)
        send3[:, span] = value.astype(bf16)
        for k in range(1, nz):
            exchange(
                2, i, send3.at[rows(zs[k]), cols(i)], recv3.at[pl.ds((k - 1) * tok, tok), cols(i)], z_nbrs[k - 1]
            ).start()
        acc[:line, span] = value

    def last_stage(i):
        span = slice(*strips[i])
        third[i].wait()
        total = acc[rows(z), span]
        for k in range(1, nz):
            total = total + recv3[(k - 1) * tok : k * tok, span].astype(f32)
        gt_out[:, span] = total.astype(bf16)

    def weight_term(k, right):
        turned = acts[k].T
        for at, size in spans(0, width):
            value = jnp.dot(turned, right[:, at : at + size], preferred_element_type=f32)
            gw[:, k * width + at : k * width + at + size] = value.astype(bf16)

    for i in range(count):
        first_stage(i)
        if i > 0:
            second_stage(i - 1)
    second_stage(count - 1)
    for d in range(1, nz):
        at_distance(d, cross_last)
    for zz in range(nz):
        arrived(0, 1, 1, zz)
        sib_send(0, 1, 1, zz)
    for rx in range(2):
        for zz in range(nz):
            arrived(1, 1, rx, zz)
            sib_send(1, 1, rx, zz)

    def other_gate_up():
        sib_arrived(0, 1)
        r = slice(replica, 2 * replica)
        gate_pre[0] = lax.dot_general(xs[r, :], w[0, :, :width], contract, preferred_element_type=f32)
        up_pre[0] = lax.dot_general(xs[r, :], wu[0], contract, preferred_element_type=f32)

    def other_acts():
        sib_arrived(1, 1)
        activate(0, 1, gate_pre.at[0], up_pre.at[0])
        weight_term(0, xs)

    fill = [other_gate_up, other_acts, functools.partial(weight_term, 1, xs), functools.partial(weight_term, 2, gs)]
    for i in range(max(count, len(fill))):
        if i < count:
            third_stage(i)
        if i < len(fill):
            fill[i]()

    def sent(p, ry, side, chunks):
        s = slot(ry, 0, 0, 0)
        move(p, s, s, z_sides[side], sz.at[(p * 2 + ry) * 2 + side], landing(p, ry, 0, 0), chunks).wait_send()

    for p in range(2):
        for ry in range(2):
            for side in range(2 if p == 0 or ry == 0 else 0):
                for depth in range(nz - 1):
                    pl.when(side_depth[side] == depth)(lambda: sent(p, ry, side, depth + 1))
            move(p, 0, 0, sib, ss.at[p, ry], sib_recv.at[p, ry], 2 * nz).wait_send()
        move(p, 0, 0, x_nbr, sx.at[p], landing(p, 0, 1, 0), nz).wait_send()
        move(p, 0, 0, y_nbr, sy.at[p], landing(p, 1, 0, 0), 2 * nz if p else nz + 1).wait_send()
    for i in range(count):
        last_stage(i)


def store_kernel(gt, gw, gt_out, gw_out, sems):
    copies = [
        pltpu.make_async_copy(gt, gt_out, sems.at[0]),
        pltpu.make_async_copy(gw, gw_out.at[0], sems.at[1]),
    ]
    for copy in copies:
        copy.start()
    for copy in copies:
        copy.wait()


def dense_shards(tokens, grad_out, route_ids, route_prob, device_expert, unit_count, expert_weights):
    tok, width = tokens.shape
    devices = lax.axis_size("expert")
    nz = devices // 4
    experts = 5 * devices // 16
    half = expert_weights.shape[1] // lax.axis_size("dp")
    spare = 128 - width % 128
    assert 3 * experts <= spare
    padded = width + spare
    replica = devices * tok
    line = nz * tok
    top = route_ids.shape[1]
    bf16, f32 = jnp.bfloat16, jnp.float32
    vmem = pltpu.VMEM
    dma = pltpu.SemaphoreType.DMA
    any_spec = pl.BlockSpec(memory_space=pl.ANY)
    smem_spec = pl.BlockSpec(memory_space=pltpu.SMEM)
    vmem_spec = pl.BlockSpec(memory_space=pltpu.VMEM)
    kept = 2 * (tok * padded + half * (-(-3 * width // 128) * 128))
    gt, gw = pl.pallas_call(
        functools.partial(split_kernel, nz, half, tok, width, experts),
        out_shape=(pltpu.VMEM((tok, width), bf16), pltpu.VMEM((half, 3 * width), bf16)),
        in_specs=[any_spec] * 5 + [smem_spec] * 2,
        out_specs=(vmem_spec, vmem_spec),
        scratch_shapes=[
            vmem((2 * replica, width), bf16), vmem((2 * replica, padded), bf16), vmem((tok, width), bf16),
            vmem((top, tok), jnp.int32), vmem((top, tok), f32),
            vmem((2, half, 3 * width), bf16), vmem((2, half, width), bf16),
            vmem((2, replica, half), f32), vmem((2, replica, half), f32),
            vmem((3, 2 * replica, half), bf16), vmem((2, replica, half), bf16),
            vmem((2 * line, width), f32),
            vmem((2 * line, width), bf16), vmem((2 * line, width), bf16),
            vmem((line, width), bf16), vmem((line, width), bf16),
            vmem((line, width), bf16), vmem(((nz - 1) * tok, width), bf16),
            dma((6,)), dma((2, 4 * nz)), dma((2, 2)), dma((8,)), dma((2,)), dma((2,)), dma((2, 2)),
            dma((3 * STRIPS,)), dma((3 * STRIPS,)),
        ],
        compiler_params=pltpu.CompilerParams(
            collective_id=0, has_side_effects=True, vmem_limit_bytes=VMEM_BYTES - kept
        ),
        name="split_backward",
    )(tokens, grad_out, expert_weights, route_ids.T, route_prob.T, device_expert, unit_count)
    return pl.pallas_call(
        store_kernel,
        out_shape=(
            jax.ShapeDtypeStruct((tok, width), bf16),
            jax.ShapeDtypeStruct((1, half, 3 * width), bf16),
        ),
        in_specs=[vmem_spec] * 2,
        out_specs=[any_spec] * 2,
        scratch_shapes=[dma((2,))],
        compiler_params=pltpu.CompilerParams(vmem_limit_bytes=1024 * 1024),
        name="store_outputs",
    )(gt, gw)


def shards(tokens, grad_out, route_ids, *rest):
    token_count = tokens.shape[0]
    capacity = token_count * route_ids.shape[1] * 4 // lax.axis_size("expert")
    form = dense_shards if capacity >= token_count else routed_shards
    return form(tokens, grad_out, route_ids, *rest)


def solution(mesh):
    in_specs = (P(AXES, None),) * 4 + (P(), P(), P("expert", None, None))
    out_specs = (P(AXES, None), P("expert", "dp", None))
    return jax.shard_map(shards, mesh=mesh, in_specs=in_specs, out_specs=out_specs, check_vma=False)
```

```python
import functools

import jax
import jax.numpy as jnp
from jax import lax
from jax.experimental import pallas as pl
from jax.experimental.pallas import tpu as pltpu
from jax.sharding import PartitionSpec as P

AXES = ("dp", "expert")


def silu_parts(preact):
    sigma = jax.nn.sigmoid(preact)
    return (preact * sigma, sigma * (1.0 + preact * (1.0 - sigma)))


def unit_work(token_rows, grad_rows, slot_weights, unit_mask):
    width = token_rows.shape[1]
    gate_rows = slot_weights[:, :width]
    up_rows = slot_weights[:, width : 2 * width]
    down_rows = slot_weights[:, 2 * width :]
    contract = (((1,), (1,)), ((), ()))
    gate_pre = lax.dot_general(token_rows, gate_rows, contract, preferred_element_type=jnp.float32)
    up_pre = lax.dot_general(token_rows, up_rows, contract, preferred_element_type=jnp.float32)
    back_grad = lax.dot_general(grad_rows, down_rows, contract, preferred_element_type=jnp.float32)
    active, slope = silu_parts(gate_pre)
    hidden = (active * up_pre * unit_mask).astype(jnp.bfloat16)
    grad_gate = (back_grad * up_pre * slope * unit_mask).astype(jnp.bfloat16)
    grad_up = (back_grad * active * unit_mask).astype(jnp.bfloat16)
    partial_value = jnp.dot(grad_gate, gate_rows, preferred_element_type=jnp.float32) + jnp.dot(
        grad_up, up_rows, preferred_element_type=jnp.float32
    )
    return (partial_value, hidden, grad_gate, grad_up)


def weight_terms(token_rows, grad_rows, hidden, grad_gate, grad_up):
    rows_first = (((0,), (0,)), ((), ()))
    return jnp.concatenate(
        [
            lax.dot_general(grad_gate, token_rows, rows_first, preferred_element_type=jnp.float32),
            lax.dot_general(grad_up, token_rows, rows_first, preferred_element_type=jnp.float32),
            lax.dot_general(hidden, grad_rows, rows_first, preferred_element_type=jnp.float32),
        ],
        axis=1,
    )


def send_back(partial_value):
    return lax.all_to_all(partial_value, "expert", split_axis=0, concat_axis=0, tiled=True)


def routed_shards(tokens, grad_out, route_ids, route_prob, device_expert, unit_count, expert_weights):
    token_count, width = tokens.shape
    top_count = route_ids.shape[1]
    devices = lax.axis_size("expert")
    experts = 5 * devices // 16
    capacity = token_count * top_count * 4 // devices
    flat_ids = route_ids.reshape(-1)
    onehot = (flat_ids[:, None] == jnp.arange(experts, dtype=jnp.int32)[None, :]).astype(jnp.int32)
    rank_of = jnp.sum(onehot * jnp.cumsum(onehot, axis=0), axis=1) - 1
    picked = (flat_ids[None, None, :] == device_expert[:, None, None]) & (
        rank_of[None, None, :] == jnp.arange(capacity, dtype=jnp.int32)[None, :, None]
    )
    picked = picked.astype(jnp.float32).reshape(devices * capacity, token_count * top_count)
    by_token = picked.reshape(devices * capacity, token_count, top_count).sum(axis=2)
    route_scale = jnp.dot(picked, route_prob.reshape(-1), precision=lax.Precision.HIGHEST)
    by_token_low = by_token.astype(jnp.bfloat16)
    sent_rows = jnp.dot(by_token_low, tokens, preferred_element_type=jnp.float32).astype(
        jnp.bfloat16
    )
    sent_grads = (
        route_scale[:, None] * jnp.dot(by_token_low, grad_out, preferred_element_type=jnp.float32)
    ).astype(jnp.bfloat16)
    outgoing = jnp.stack([sent_rows, sent_grads], axis=1).reshape(devices, capacity, 2, width)
    position = lax.axis_index("expert")
    unit_limit = lax.dynamic_index_in_dim(unit_count, position, keepdims=False)
    slot_weights = expert_weights[0]
    slot_units = slot_weights.shape[0]
    unit_mask = (jnp.arange(slot_units, dtype=jnp.int32) < unit_limit).astype(jnp.float32)
    arrived = lax.all_to_all(outgoing, "expert", split_axis=0, concat_axis=0, tiled=True)
    row_pairs = arrived.reshape(-1, 2, width)
    partial_value, hidden, grad_gate, grad_up = unit_work(
        row_pairs[:, 0], row_pairs[:, 1], slot_weights, unit_mask
    )
    leading = (arrived.shape[0], arrived.shape[1])
    returned, all_rows, hidden, grad_gate, grad_up = (
        send_back(partial_value.reshape(leading + (width,))),
        arrived,
        hidden.reshape(leading + (slot_units,)),
        grad_gate.reshape(leading + (slot_units,)),
        grad_up.reshape(leading + (slot_units,)),
    )
    row_pairs = all_rows.reshape(-1, 2, width)
    token_rows = row_pairs[:, 0]
    grad_rows = row_pairs[:, 1]
    hidden = hidden.reshape(-1, slot_units)
    grad_gate = grad_gate.reshape(-1, slot_units)
    grad_up = grad_up.reshape(-1, slot_units)
    term_block = weight_terms(token_rows, grad_rows, hidden, grad_gate, grad_up)
    grad_weights = lax.psum_scatter(term_block, "dp", scatter_dimension=0, tiled=True)
    parts = returned.reshape(devices * capacity, width)
    grad_tokens = lax.dot_general(
        by_token,
        parts,
        (((0,), (0,)), ((), ())),
        precision=lax.Precision.HIGHEST,
        preferred_element_type=jnp.float32,
    )
    return (grad_tokens.astype(jnp.bfloat16), grad_weights.astype(jnp.bfloat16)[None])


MESH = pl.DeviceIdType.MESH
STEP = 256
STRIPS = 6
FILLS = (1, 2, 3, 5, 6, 8)
VMEM_BYTES = 67043328


def split_kernel(
    nz, half, tok, width, experts,
    x_in, g_in, w_in, ids_in, prob_in, expert_ref, limit_ref, gt_out, gw,
    xs, gs, own_g, ids, prob, w, wu, gate, up, slope, own_acts, acts, turned, acc,
    send1, recv1, send2, recv2, send3, recv3,
    local_sem, recv_sem, sib_recv, sz, sx, sy, ss, rs_send, rs_recv,
):
    f32, bf16 = jnp.float32, jnp.bfloat16
    y = lax.axis_index("dp")
    position = lax.axis_index("expert")
    z, x, c = position // 4, (position // 2) % 2, position % 2

    def place(yy, zz, xx, cc):
        return (yy, zz * 4 + xx * 2 + cc)

    zs = [lax.rem(z + k, nz) for k in range(nz)]
    x_nbr, y_nbr, sib = place(y, z, 1 - x, c), place(1 - y, z, x, c), place(y, z, x, 1 - c)
    z_nbrs = [place(y, zs[k], x, c) for k in range(1, nz)]
    z_sides = (place(y, lax.rem(z + nz - 1, nz), x, c), place(y, lax.rem(z + 1, nz), x, c))
    has_side = (z > 0, z < nz - 1)
    side_depth = (nz - 1 - z, z)
    barrier = pltpu.get_barrier_semaphore()
    for peer in (x_nbr, y_nbr, sib):
        pl.semaphore_signal(barrier, inc=1, device_id=peer, device_id_type=MESH)
    for side in range(2):
        pl.when(has_side[side])(
            lambda: pl.semaphore_signal(barrier, inc=1, device_id=z_sides[side], device_id_type=MESH)
        )

    line = nz * tok
    side_rows = 2 * line
    replica = 2 * side_rows

    def slot(ry, rc, rx, zz):
        return ((ry * 2 + rc) * 2 + rx) * nz + zz

    def rows(s, count=1):
        return pl.ds(pl.multiple_of(s * tok, tok), count * tok)

    start = slot(0, 0, 0, z)
    own_x = pltpu.make_async_copy(x_in, xs.at[rows(start)], local_sem.at[0])
    load_g = pltpu.make_async_copy(g_in, own_g, local_sem.at[1])
    load_ids = pltpu.make_async_copy(ids_in, ids, local_sem.at[2])
    load_prob = pltpu.make_async_copy(prob_in, prob, local_sem.at[3])
    for copy in (own_x, load_ids, load_prob, load_g):
        copy.start()
    load_w = []
    for h in range(2):
        first = pl.multiple_of((y if h == 0 else 1 - y) * half, 16)
        load_w.append(pltpu.make_async_copy(w_in.at[0, pl.ds(first, half)], w.at[pl.ds(h * half, half)], local_sem.at[4 + h]))
        load_w[h].start()

    spare = gs.shape[1] - width
    lane = lax.broadcasted_iota(jnp.int32, (tok, spare), 1)
    diagonal = lax.broadcasted_iota(jnp.int32, (tok, tok), 0) == lax.broadcasted_iota(jnp.int32, (tok, tok), 1)

    def column(row):
        return jnp.sum(jnp.where(diagonal, jnp.broadcast_to(row, (tok, tok)), 0.0), axis=1, keepdims=True)

    load_ids.wait()
    load_prob.wait()
    scales = jnp.zeros((tok, spare), f32)
    which = (lane % experts).astype(f32)
    for k in range(ids.shape[0]):
        named = column(ids[k : k + 1, :].astype(f32))
        scales += jnp.where(named == which, column(prob[k : k + 1, :]), 0.0)
    high = scales.astype(bf16).astype(f32)
    middle = (scales - high).astype(bf16).astype(f32)
    term = lane // experts
    packed = jnp.where(term == 0, high, jnp.where(term == 1, middle, scales - high - middle))
    load_g.wait()
    gs[rows(start), :width] = own_g[...]
    gs[rows(start), width:] = jnp.where(term < 3, packed, 0.0).astype(bf16)
    own_x.wait()
    at_end = (z == 0) | (z == nz - 1)
    pl.semaphore_wait(barrier, jnp.where(at_end, 4, 5))

    bufs = (xs, gs)

    def move(p, src, dst, target, send, recv, count=1):
        return pltpu.make_async_remote_copy(
            src_ref=bufs[p].at[rows(src, count)], dst_ref=bufs[p].at[rows(dst, count)],
            send_sem=send, recv_sem=recv, device_id=target, device_id_type=MESH,
        )

    def landing(p, ry, rx, zz):
        return recv_sem.at[p, (ry * 2 + rx) * nz + zz]

    def arrived(p, ry, rx, zz):
        s = slot(ry, 0, rx, zz)
        move(p, s, s, sib, ss.at[p, ry], landing(p, ry, rx, zz)).wait_recv()

    def z_send(p, ry, zz, side):
        s = slot(ry, 0, 0, zz)
        move(p, s, s, z_sides[side], sz.at[(p * 2 + ry) * 2 + side], landing(p, ry, 0, zz)).start()

    def x_send(p, zz):
        move(p, slot(0, 0, 0, zz), slot(0, 0, 1, zz), x_nbr, sx.at[p], landing(p, 0, 1, zz)).start()

    def y_send(p, rx, zz):
        move(p, slot(0, 0, rx, zz), slot(1, 0, rx, zz), y_nbr, sy.at[p], landing(p, 1, rx, zz)).start()

    def sib_send(p, ry, rx, zz):
        move(p, slot(ry, 0, rx, zz), slot(ry, 1, rx, zz), sib, ss.at[p, ry], sib_recv.at[p, ry]).start()

    def sib_arrived(p, ry):
        s = slot(ry, 1, 0, 0)
        move(p, s, s, sib, ss.at[p, ry], sib_recv.at[p, ry], 2 * nz).wait_recv()

    def at_distance(d, act):
        for side, zz in ((0, z - d), (1, z + d)):
            pl.when((zz >= 0) & (zz < nz))(functools.partial(act, side, zz))

    def from_z(d, side, zz):
        for p in range(2):
            arrived(p, 0, 0, zz)
            pl.when(has_side[1 - side])(lambda: z_send(p, 0, zz, 1 - side))
            x_send(p, zz)
            if p == 1 and d > 1:
                y_send(1, 0, zz)
            sib_send(p, 0, 0, zz)

    def relay_x(p, zz):
        arrived(p, 0, 1, zz)
        sib_send(p, 0, 1, zz)

    def relay_xy(p, zz):
        relay_x(p, zz)
        y_send(p, 1, zz)

    def x_cross(p):
        move(p, slot(1, 0, 0, z), slot(1, 0, 1, z), x_nbr, sx.at[p], landing(p, 1, 1, z)).start()

    def z_cross(side):
        for p in range(2):
            z_send(p, 1, z, side)

    def cross_relay(side, zz):
        def go():
            arrived(0, 1, 0, zz)
            z_send(0, 1, zz, 1 - side)
            sib_send(0, 1, 0, zz)
        pl.when(has_side[1 - side])(go)

    def cross_last(side, zz):
        def go():
            arrived(0, 1, 0, zz)
            sib_send(0, 1, 0, zz)
        pl.when(jnp.logical_not(has_side[1 - side]))(go)

    for p in range(2):
        for side in range(2):
            pl.when(has_side[side])(lambda: z_send(p, 0, z, side))
        x_send(p, z)
        y_send(p, 0, z)
        sib_send(p, 0, 0, z)
    late = nz - 2
    for d in range(1, nz):
        at_distance(d, functools.partial(from_z, d))
        if d == 1:
            for p in range(2):
                relay_x(p, z)
            for p in range(2):
                arrived(p, 1, 0, z)
                sib_send(p, 1, 0, z)
        elif d - 1 < late:
            for p in range(2):
                at_distance(d - 1, lambda side, zz: relay_xy(p, zz))
        for side in range(2):
            ready = side_depth[side] <= 1 if d == 1 else side_depth[side] == d
            pl.when(has_side[side] & ready)(lambda: z_cross(side))

    for p in range(2):
        x_cross(p)

    expert = expert_ref[position]
    lane = lax.broadcasted_iota(jnp.int32, (1, 128), 1) - (128 - spare)
    sel = jnp.where((lane >= 0) & (lane < 3 * experts) & (lane % experts == expert), 1.0, 0.0)
    contract = (((1,), (1,)), ((), ()))
    tail = width // 128 * 128

    for h in range(2):
        load_w[h].wait()
        wu[h * half : (h + 1) * half] = w[h * half : (h + 1) * half, width : 2 * width]
    at_distance(1, cross_relay)
    for d in range(late, nz):
        at_distance(d, lambda side, zz: relay_xy(0, zz))
    sib_arrived(0, 0)
    gate[...] = lax.dot_general(xs[:replica, :], w[:, :width], contract, preferred_element_type=f32)
    for d in range(late, nz):
        at_distance(d, lambda side, zz: relay_xy(1, zz))
    for d in range(2, nz - 1):
        at_distance(d, cross_relay)
    up[...] = lax.dot_general(xs[:replica, :], wu[...], contract, preferred_element_type=f32)

    def derive(units):
        lane = lax.broadcasted_iota(jnp.int32, (1, units), 1)
        unit = jnp.where(lane < half, lane + y * half, lane - y * half)
        g = gate[:, :units]
        live = jnp.broadcast_to(jnp.where(unit < limit_ref[position], 1.0, 0.0), g.shape) > 0.0
        sigma = 1.0 / (1.0 + jnp.exp(-g))
        gate[:, :units] = jnp.where(live, g * sigma, 0.0)
        slope[:, :units] = jnp.where(live, up[:, :units] * (sigma * (1.0 + g * (1.0 - sigma))), 0.0)

    def scale_of(r):
        return jnp.sum(gs[r, tail:].astype(f32) * sel, axis=1, keepdims=True)

    def back(r, units):
        return scale_of(r) * lax.dot_general(
            gs[r, :width], w[:units, 2 * width :], contract, preferred_element_type=f32
        )

    mine, other = slice(0, replica), slice(replica, 2 * replica)
    derive(2 * half)
    sib_arrived(1, 0)
    b = back(mine, 2 * half)
    own_acts[0] = (b * slope[...]).astype(bf16)
    own_acts[1] = (b * gate[...]).astype(bf16)

    quarter = (width // 128 + STRIPS) // STRIPS * 128
    strips = [(at, min(at + quarter, width)) for at in range(0, width, quarter)]
    count = len(strips)

    def spans(begin, end):
        return [(at, min(STEP, end - at)) for at in range(begin, end, STEP)]

    def exchange(stage, i, src, dst, target):
        return pltpu.make_async_remote_copy(
            src_ref=src, dst_ref=dst, send_sem=rs_send.at[stage * count + i],
            recv_sem=rs_recv.at[stage * count + i], device_id=target, device_id_type=MESH,
        )

    def cols(i):
        begin, end = strips[i]
        return pl.ds(begin, end - begin)

    core = [exchange(0, i, send1.at[:, cols(i)], recv1.at[:, cols(i)], sib) for i in range(count)]
    second = [exchange(1, i, send2.at[:, cols(i)], recv2.at[:, cols(i)], x_nbr) for i in range(count)]
    third = [
        exchange(2, i, send3.at[pl.ds(0, (nz - 1) * tok), cols(i)], recv3.at[:, cols(i)], z_nbrs[0])
        for i in range(count)
    ]

    def first_stage(i):
        for at, size in spans(*strips[i]):
            span = slice(at, at + size)
            value = jnp.dot(own_acts[0], w[:, span], preferred_element_type=f32)
            value += jnp.dot(own_acts[1], wu[:, span], preferred_element_type=f32)
            send1[:, span] = value[side_rows:].astype(bf16)
            acc[:, span] = value[:side_rows]
        core[i].start()

    def second_stage(i):
        span = slice(*strips[i])
        core[i].wait()
        send2[:, span] = (acc[line:, span] + recv1[line:, span].astype(f32)).astype(bf16)
        second[i].start()
        acc[:line, span] = acc[:line, span] + recv1[:line, span].astype(f32)

    def third_stage(i):
        span = slice(*strips[i])
        second[i].wait()
        value = acc[:line, span] + recv2[:, span].astype(f32)
        send3[:, span] = value.astype(bf16)
        for k in range(1, nz):
            exchange(
                2, i, send3.at[rows(zs[k]), cols(i)], recv3.at[pl.ds((k - 1) * tok, tok), cols(i)], z_nbrs[k - 1]
            ).start()
        acc[:line, span] = value

    def last_stage(i):
        span = slice(*strips[i])
        third[i].wait()
        total = acc[rows(z), span]
        for k in range(1, nz):
            total = total + recv3[(k - 1) * tok : k * tok, span].astype(f32)
        gt_out[:, span] = total.astype(bf16)

    cuts = spans(0, width)
    middle = len(cuts) // 2

    def weight_term(k, right, part):
        if part == 0:
            turned[...] = acts[k].T
        for at, size in cuts[middle:] if part else cuts[:middle]:
            value = jnp.dot(turned[...], right[:, at : at + size], preferred_element_type=f32)
            gw[:, k * width + at : k * width + at + size] = value.astype(bf16)

    def keep_own():
        for k in range(2):
            acts[k, mine, :] = own_acts[k, :, :half]
        acts[2, mine, :] = (gate[:, :half] * up[:, :half] * scale_of(mine)).astype(bf16)

    def pass_rows():
        for d in range(1, nz):
            at_distance(d, cross_last)
        for zz in range(nz):
            arrived(0, 1, 1, zz)
            sib_send(0, 1, 1, zz)

    def pass_column(side, zz):
        arrived(1, 1, 0, zz)
        sib_send(1, 1, 0, zz)

    def pass_grads():
        for d in range(1, nz):
            at_distance(d, pass_column)
        for zz in range(nz):
            arrived(1, 1, 1, zz)
            sib_send(1, 1, 1, zz)

    def other_gate():
        sib_arrived(0, 1)
        gate[:, :half] = lax.dot_general(xs[other, :], w[:half, :width], contract, preferred_element_type=f32)

    def other_up():
        up[:, :half] = lax.dot_general(xs[other, :], wu[:half], contract, preferred_element_type=f32)
        derive(half)

    def other_back():
        sib_arrived(1, 1)
        b = back(other, half)
        acts[0, other, :] = (b * slope[:, :half]).astype(bf16)
        acts[1, other, :] = (b * gate[:, :half]).astype(bf16)
        acts[2, other, :] = (gate[:, :half] * up[:, :half] * scale_of(other)).astype(bf16)

    fill = [pass_rows, pass_grads, keep_own, other_gate, other_up, other_back]
    for k, right in enumerate((xs, xs, gs)):
        for part in range(2):
            fill.append(functools.partial(weight_term, k, right, part))

    for i in range(count):
        first_stage(i)
        if i > 0:
            second_stage(i - 1)
    second_stage(count - 1)
    done = 0
    for i in range(-1, count):
        if i >= 0:
            third_stage(i)
        upto = FILLS[i + 1] if i + 1 < count else len(fill)
        for act in fill[done:upto]:
            act()
        done = upto

    def sent(p, ry, side, chunks):
        s = slot(ry, 0, 0, 0)
        move(p, s, s, z_sides[side], sz.at[(p * 2 + ry) * 2 + side], landing(p, ry, 0, 0), chunks).wait_send()

    def to_y(p, chunks):
        move(p, 0, 0, y_nbr, sy.at[p], landing(p, 1, 0, 0), chunks).wait_send()

    for p in range(2):
        for ry in range(2):
            for side in range(2):
                if p == 1 and ry == 1:
                    pl.when(has_side[side])(lambda: sent(p, ry, side, 1))
                    continue
                for depth in range(nz - 1):
                    pl.when(side_depth[side] == depth)(lambda: sent(p, ry, side, depth + 1))
            move(p, 0, 0, sib, ss.at[p, ry], sib_recv.at[p, ry], 2 * nz).wait_send()
        move(p, 0, 0, x_nbr, sx.at[p], landing(p, 0, 1, 0), nz + 1).wait_send()
        if p == 0:
            to_y(p, nz)
        else:
            pl.when(at_end)(lambda: to_y(p, 2 * nz - 2))
            pl.when(jnp.logical_not(at_end))(lambda: to_y(p, 2 * nz - 3))
    for i in range(count):
        last_stage(i)


def store_kernel(gt, gw, gt_out, gw_out, sems):
    copies = [
        pltpu.make_async_copy(gt, gt_out, sems.at[0]),
        pltpu.make_async_copy(gw, gw_out.at[0], sems.at[1]),
    ]
    for copy in copies:
        copy.start()
    for copy in copies:
        copy.wait()


def dense_shards(tokens, grad_out, route_ids, route_prob, device_expert, unit_count, expert_weights):
    tok, width = tokens.shape
    devices = lax.axis_size("expert")
    nz = devices // 4
    experts = 5 * devices // 16
    half = expert_weights.shape[1] // lax.axis_size("dp")
    spare = 128 - width % 128
    assert 3 * experts <= spare
    padded = width + spare
    replica = devices * tok
    line = nz * tok
    top = route_ids.shape[1]
    bf16, f32 = jnp.bfloat16, jnp.float32
    vmem = pltpu.VMEM
    dma = pltpu.SemaphoreType.DMA
    any_spec = pl.BlockSpec(memory_space=pl.ANY)
    smem_spec = pl.BlockSpec(memory_space=pltpu.SMEM)
    vmem_spec = pl.BlockSpec(memory_space=pltpu.VMEM)
    kept = 2 * (tok * padded + half * (-(-3 * width // 128) * 128))
    gt, gw = pl.pallas_call(
        functools.partial(split_kernel, nz, half, tok, width, experts),
        out_shape=(pltpu.VMEM((tok, width), bf16), pltpu.VMEM((half, 3 * width), bf16)),
        in_specs=[any_spec] * 5 + [smem_spec] * 2,
        out_specs=(vmem_spec, vmem_spec),
        scratch_shapes=[
            vmem((2 * replica, width), bf16), vmem((2 * replica, padded), bf16), vmem((tok, width), bf16),
            vmem((top, tok), jnp.int32), vmem((top, tok), f32),
            vmem((2 * half, 3 * width), bf16), vmem((2 * half, width), bf16),
            vmem((replica, 2 * half), f32), vmem((replica, 2 * half), f32), vmem((replica, 2 * half), f32),
            vmem((2, replica, 2 * half), bf16), vmem((3, 2 * replica, half), bf16), vmem((half, 2 * replica), bf16),
            vmem((2 * line, width), f32),
            vmem((2 * line, width), bf16), vmem((2 * line, width), bf16),
            vmem((line, width), bf16), vmem((line, width), bf16),
            vmem((line, width), bf16), vmem(((nz - 1) * tok, width), bf16),
            dma((6,)), dma((2, 4 * nz)), dma((2, 2)), dma((8,)), dma((2,)), dma((2,)), dma((2, 2)),
            dma((3 * STRIPS,)), dma((3 * STRIPS,)),
        ],
        compiler_params=pltpu.CompilerParams(
            collective_id=0, has_side_effects=True, vmem_limit_bytes=VMEM_BYTES - kept
        ),
        name="split_backward",
    )(tokens, grad_out, expert_weights, route_ids.T, route_prob.T, device_expert, unit_count)
    return pl.pallas_call(
        store_kernel,
        out_shape=(
            jax.ShapeDtypeStruct((tok, width), bf16),
            jax.ShapeDtypeStruct((1, half, 3 * width), bf16),
        ),
        in_specs=[vmem_spec] * 2,
        out_specs=[any_spec] * 2,
        scratch_shapes=[dma((2,))],
        compiler_params=pltpu.CompilerParams(vmem_limit_bytes=1024 * 1024),
        name="store_outputs",
    )(gt, gw)


def shards(tokens, grad_out, route_ids, *rest):
    token_count = tokens.shape[0]
    capacity = token_count * route_ids.shape[1] * 4 // lax.axis_size("expert")
    form = dense_shards if capacity >= token_count else routed_shards
    return form(tokens, grad_out, route_ids, *rest)


def solution(mesh):
    in_specs = (P(AXES, None),) * 4 + (P(), P(), P("expert", None, None))
    out_specs = (P(AXES, None), P("expert", "dp", None))
    return jax.shard_map(shards, mesh=mesh, in_specs=in_specs, out_specs=out_specs, check_vma=False)
```

```python
import functools

import jax
import jax.numpy as jnp
from jax import lax
from jax.experimental import pallas as pl
from jax.experimental.pallas import tpu as pltpu
from jax.sharding import PartitionSpec as P

AXES = ("dp", "expert")


def silu_parts(preact):
    sigma = jax.nn.sigmoid(preact)
    return (preact * sigma, sigma * (1.0 + preact * (1.0 - sigma)))


def unit_work(token_rows, grad_rows, slot_weights, unit_mask):
    width = token_rows.shape[1]
    gate_rows = slot_weights[:, :width]
    up_rows = slot_weights[:, width : 2 * width]
    down_rows = slot_weights[:, 2 * width :]
    contract = (((1,), (1,)), ((), ()))
    gate_pre = lax.dot_general(token_rows, gate_rows, contract, preferred_element_type=jnp.float32)
    up_pre = lax.dot_general(token_rows, up_rows, contract, preferred_element_type=jnp.float32)
    back_grad = lax.dot_general(grad_rows, down_rows, contract, preferred_element_type=jnp.float32)
    active, slope = silu_parts(gate_pre)
    hidden = (active * up_pre * unit_mask).astype(jnp.bfloat16)
    grad_gate = (back_grad * up_pre * slope * unit_mask).astype(jnp.bfloat16)
    grad_up = (back_grad * active * unit_mask).astype(jnp.bfloat16)
    partial_value = jnp.dot(grad_gate, gate_rows, preferred_element_type=jnp.float32) + jnp.dot(
        grad_up, up_rows, preferred_element_type=jnp.float32
    )
    return (partial_value, hidden, grad_gate, grad_up)


def weight_terms(token_rows, grad_rows, hidden, grad_gate, grad_up):
    rows_first = (((0,), (0,)), ((), ()))
    return jnp.concatenate(
        [
            lax.dot_general(grad_gate, token_rows, rows_first, preferred_element_type=jnp.float32),
            lax.dot_general(grad_up, token_rows, rows_first, preferred_element_type=jnp.float32),
            lax.dot_general(hidden, grad_rows, rows_first, preferred_element_type=jnp.float32),
        ],
        axis=1,
    )


def send_back(partial_value):
    return lax.all_to_all(partial_value, "expert", split_axis=0, concat_axis=0, tiled=True)


def routed_shards(tokens, grad_out, route_ids, route_prob, device_expert, unit_count, expert_weights):
    token_count, width = tokens.shape
    top_count = route_ids.shape[1]
    devices = lax.axis_size("expert")
    experts = 5 * devices // 16
    capacity = token_count * top_count * 4 // devices
    flat_ids = route_ids.reshape(-1)
    onehot = (flat_ids[:, None] == jnp.arange(experts, dtype=jnp.int32)[None, :]).astype(jnp.int32)
    rank_of = jnp.sum(onehot * jnp.cumsum(onehot, axis=0), axis=1) - 1
    picked = (flat_ids[None, None, :] == device_expert[:, None, None]) & (
        rank_of[None, None, :] == jnp.arange(capacity, dtype=jnp.int32)[None, :, None]
    )
    picked = picked.astype(jnp.float32).reshape(devices * capacity, token_count * top_count)
    by_token = picked.reshape(devices * capacity, token_count, top_count).sum(axis=2)
    route_scale = jnp.dot(picked, route_prob.reshape(-1), precision=lax.Precision.HIGHEST)
    by_token_low = by_token.astype(jnp.bfloat16)
    sent_rows = jnp.dot(by_token_low, tokens, preferred_element_type=jnp.float32).astype(
        jnp.bfloat16
    )
    sent_grads = (
        route_scale[:, None] * jnp.dot(by_token_low, grad_out, preferred_element_type=jnp.float32)
    ).astype(jnp.bfloat16)
    outgoing = jnp.stack([sent_rows, sent_grads], axis=1).reshape(devices, capacity, 2, width)
    position = lax.axis_index("expert")
    unit_limit = lax.dynamic_index_in_dim(unit_count, position, keepdims=False)
    slot_weights = expert_weights[0]
    slot_units = slot_weights.shape[0]
    unit_mask = (jnp.arange(slot_units, dtype=jnp.int32) < unit_limit).astype(jnp.float32)
    arrived = lax.all_to_all(outgoing, "expert", split_axis=0, concat_axis=0, tiled=True)
    row_pairs = arrived.reshape(-1, 2, width)
    partial_value, hidden, grad_gate, grad_up = unit_work(
        row_pairs[:, 0], row_pairs[:, 1], slot_weights, unit_mask
    )
    leading = (arrived.shape[0], arrived.shape[1])
    returned, all_rows, hidden, grad_gate, grad_up = (
        send_back(partial_value.reshape(leading + (width,))),
        arrived,
        hidden.reshape(leading + (slot_units,)),
        grad_gate.reshape(leading + (slot_units,)),
        grad_up.reshape(leading + (slot_units,)),
    )
    row_pairs = all_rows.reshape(-1, 2, width)
    token_rows = row_pairs[:, 0]
    grad_rows = row_pairs[:, 1]
    hidden = hidden.reshape(-1, slot_units)
    grad_gate = grad_gate.reshape(-1, slot_units)
    grad_up = grad_up.reshape(-1, slot_units)
    term_block = weight_terms(token_rows, grad_rows, hidden, grad_gate, grad_up)
    grad_weights = lax.psum_scatter(term_block, "dp", scatter_dimension=0, tiled=True)
    parts = returned.reshape(devices * capacity, width)
    grad_tokens = lax.dot_general(
        by_token,
        parts,
        (((0,), (0,)), ((), ())),
        precision=lax.Precision.HIGHEST,
        preferred_element_type=jnp.float32,
    )
    return (grad_tokens.astype(jnp.bfloat16), grad_weights.astype(jnp.bfloat16)[None])


MESH = pl.DeviceIdType.MESH
STEP = 256
STRIPS = 6
FILLS = (1, 2, 3, 5, 6, 8)
VMEM_BYTES = 67043328


def split_kernel(
    nz, half, tok, width, experts,
    x_in, g_in, w_in, ids_in, prob_in, expert_in, limit_in, gt_out, gw,
    xs, gs, own_g, ids, prob, expert_ref, limit_ref, w, wu, gate, up, slope, own_acts, acts, turned, acc,
    send1, recv1, send2, recv2, send3, recv3,
    local_sem, recv_sem, sib_recv, sz, sx, sy, ss, rs_send, rs_recv,
):
    f32, bf16 = jnp.float32, jnp.bfloat16
    y = lax.axis_index("dp")
    position = lax.axis_index("expert")
    z, x, c = position // 4, (position // 2) % 2, position % 2

    def place(yy, zz, xx, cc):
        return (yy, zz * 4 + xx * 2 + cc)

    zs = [lax.rem(z + k, nz) for k in range(nz)]
    x_nbr, y_nbr, sib = place(y, z, 1 - x, c), place(1 - y, z, x, c), place(y, z, x, 1 - c)
    z_nbrs = [place(y, zs[k], x, c) for k in range(1, nz)]
    z_sides = (place(y, lax.rem(z + nz - 1, nz), x, c), place(y, lax.rem(z + 1, nz), x, c))
    has_side = (z > 0, z < nz - 1)
    side_depth = (nz - 1 - z, z)
    barrier = pltpu.get_barrier_semaphore()
    for peer in (x_nbr, y_nbr, sib):
        pl.semaphore_signal(barrier, inc=1, device_id=peer, device_id_type=MESH)
    for side in range(2):
        pl.when(has_side[side])(
            lambda: pl.semaphore_signal(barrier, inc=1, device_id=z_sides[side], device_id_type=MESH)
        )

    line = nz * tok
    side_rows = 2 * line
    replica = 2 * side_rows

    def slot(ry, rc, rx, zz):
        return ((ry * 2 + rc) * 2 + rx) * nz + zz

    def rows(s, count=1):
        return pl.ds(pl.multiple_of(s * tok, tok), count * tok)

    start = slot(0, 0, 0, z)
    own_x = pltpu.make_async_copy(x_in, xs.at[rows(start)], local_sem.at[0])
    load_g = pltpu.make_async_copy(g_in, own_g, local_sem.at[1])
    load_ids = pltpu.make_async_copy(ids_in, ids, local_sem.at[2])
    load_prob = pltpu.make_async_copy(prob_in, prob, local_sem.at[3])
    load_expert = pltpu.make_async_copy(expert_in, expert_ref, local_sem.at[6])
    load_limit = pltpu.make_async_copy(limit_in, limit_ref, local_sem.at[7])
    for copy in (own_x, load_ids, load_prob, load_g, load_expert, load_limit):
        copy.start()
    load_w = []
    for h in range(2):
        first = pl.multiple_of((y if h == 0 else 1 - y) * half, 16)
        load_w.append(pltpu.make_async_copy(w_in.at[0, pl.ds(first, half)], w.at[pl.ds(h * half, half)], local_sem.at[4 + h]))
        load_w[h].start()

    spare = gs.shape[1] - width
    lane = lax.broadcasted_iota(jnp.int32, (tok, spare), 1)
    diagonal = lax.broadcasted_iota(jnp.int32, (tok, tok), 0) == lax.broadcasted_iota(jnp.int32, (tok, tok), 1)

    def column(row):
        return jnp.sum(jnp.where(diagonal, jnp.broadcast_to(row, (tok, tok)), 0.0), axis=1, keepdims=True)

    load_ids.wait()
    load_prob.wait()
    scales = jnp.zeros((tok, spare), f32)
    which = (lane % experts).astype(f32)
    for k in range(ids.shape[0]):
        named = column(ids[k : k + 1, :].astype(f32))
        scales += jnp.where(named == which, column(prob[k : k + 1, :]), 0.0)
    high = scales.astype(bf16).astype(f32)
    middle = (scales - high).astype(bf16).astype(f32)
    term = lane // experts
    packed = jnp.where(term == 0, high, jnp.where(term == 1, middle, scales - high - middle))
    load_g.wait()
    gs[rows(start), :width] = own_g[...]
    gs[rows(start), width:] = jnp.where(term < 3, packed, 0.0).astype(bf16)
    own_x.wait()
    at_end = (z == 0) | (z == nz - 1)
    pl.semaphore_wait(barrier, jnp.where(at_end, 4, 5))

    bufs = (xs, gs)

    def move(p, src, dst, target, send, recv, count=1):
        return pltpu.make_async_remote_copy(
            src_ref=bufs[p].at[rows(src, count)], dst_ref=bufs[p].at[rows(dst, count)],
            send_sem=send, recv_sem=recv, device_id=target, device_id_type=MESH,
        )

    def landing(p, ry, rx, zz):
        return recv_sem.at[p, (ry * 2 + rx) * nz + zz]

    def arrived(p, ry, rx, zz):
        s = slot(ry, 0, rx, zz)
        move(p, s, s, sib, ss.at[p, ry], landing(p, ry, rx, zz)).wait_recv()

    def z_send(p, ry, zz, side):
        s = slot(ry, 0, 0, zz)
        move(p, s, s, z_sides[side], sz.at[(p * 2 + ry) * 2 + side], landing(p, ry, 0, zz)).start()

    def x_send(p, zz):
        move(p, slot(0, 0, 0, zz), slot(0, 0, 1, zz), x_nbr, sx.at[p], landing(p, 0, 1, zz)).start()

    def y_send(p, rx, zz):
        move(p, slot(0, 0, rx, zz), slot(1, 0, rx, zz), y_nbr, sy.at[p], landing(p, 1, rx, zz)).start()

    def sib_send(p, ry, rx, zz):
        move(p, slot(ry, 0, rx, zz), slot(ry, 1, rx, zz), sib, ss.at[p, ry], sib_recv.at[p, ry]).start()

    def sib_arrived(p, ry):
        s = slot(ry, 1, 0, 0)
        move(p, s, s, sib, ss.at[p, ry], sib_recv.at[p, ry], 2 * nz).wait_recv()

    def at_distance(d, act):
        for side, zz in ((0, z - d), (1, z + d)):
            pl.when((zz >= 0) & (zz < nz))(functools.partial(act, side, zz))

    def from_z(d, side, zz):
        for p in range(2):
            arrived(p, 0, 0, zz)
            pl.when(has_side[1 - side])(lambda: z_send(p, 0, zz, 1 - side))
            x_send(p, zz)
            if p == 1 and d > 1:
                y_send(1, 0, zz)
            sib_send(p, 0, 0, zz)

    def relay_x(p, zz):
        arrived(p, 0, 1, zz)
        sib_send(p, 0, 1, zz)

    def relay_xy(p, zz):
        relay_x(p, zz)
        y_send(p, 1, zz)

    def x_cross(p):
        move(p, slot(1, 0, 0, z), slot(1, 0, 1, z), x_nbr, sx.at[p], landing(p, 1, 1, z)).start()

    def z_cross(side):
        for p in range(2):
            z_send(p, 1, z, side)

    def cross_relay(side, zz):
        def go():
            arrived(0, 1, 0, zz)
            z_send(0, 1, zz, 1 - side)
            sib_send(0, 1, 0, zz)
        pl.when(has_side[1 - side])(go)

    def cross_last(side, zz):
        def go():
            arrived(0, 1, 0, zz)
            sib_send(0, 1, 0, zz)
        pl.when(jnp.logical_not(has_side[1 - side]))(go)

    for p in range(2):
        for side in range(2):
            pl.when(has_side[side])(lambda: z_send(p, 0, z, side))
        x_send(p, z)
        y_send(p, 0, z)
        sib_send(p, 0, 0, z)
    late = nz - 2
    for d in range(1, nz):
        at_distance(d, functools.partial(from_z, d))
        if d == 1:
            for p in range(2):
                relay_xy(p, z)
            for p in range(2):
                arrived(p, 1, 0, z)
                sib_send(p, 1, 0, z)
            for h in range(2):
                load_w[h].wait()
                wu[h * half : (h + 1) * half] = w[h * half : (h + 1) * half, width : 2 * width]
        elif d - 1 < late:
            for p in range(2):
                at_distance(d - 1, lambda side, zz: relay_xy(p, zz))
        for side in range(2):
            ready = side_depth[side] <= 1 if d == 1 else side_depth[side] == d
            pl.when(has_side[side] & ready)(lambda: z_cross(side))


    load_expert.wait()
    load_limit.wait()
    expert = expert_ref[position]
    lane = lax.broadcasted_iota(jnp.int32, (1, 128), 1) - (128 - spare)
    sel = jnp.where((lane >= 0) & (lane < 3 * experts) & (lane % experts == expert), 1.0, 0.0)
    contract = (((1,), (1,)), ((), ()))
    tail = width // 128 * 128

    at_distance(1, cross_relay)
    for d in range(late, nz):
        at_distance(d, lambda side, zz: relay_xy(0, zz))
    sib_arrived(0, 0)
    gate[...] = lax.dot_general(xs[:replica, :], w[:, :width], contract, preferred_element_type=f32)
    for d in range(late, nz):
        at_distance(d, lambda side, zz: relay_xy(1, zz))
    for d in range(2, nz - 1):
        at_distance(d, cross_relay)
    up[...] = lax.dot_general(xs[:replica, :], wu[...], contract, preferred_element_type=f32)

    def derive(units):
        lane = lax.broadcasted_iota(jnp.int32, (1, units), 1)
        unit = jnp.where(lane < half, lane + y * half, lane - y * half)
        g = gate[:, :units]
        live = jnp.broadcast_to(jnp.where(unit < limit_ref[position], 1.0, 0.0), g.shape) > 0.0
        sigma = 1.0 / (1.0 + jnp.exp(-g))
        gate[:, :units] = jnp.where(live, g * sigma, 0.0)
        slope[:, :units] = jnp.where(live, up[:, :units] * (sigma * (1.0 + g * (1.0 - sigma))), 0.0)

    def scale_of(r):
        return jnp.sum(gs[r, tail:].astype(f32) * sel, axis=1, keepdims=True)

    def back(r, units):
        return scale_of(r) * lax.dot_general(
            gs[r, :width], w[:units, 2 * width :], contract, preferred_element_type=f32
        )

    mine, other = slice(0, replica), slice(replica, 2 * replica)
    derive(2 * half)
    sib_arrived(1, 0)
    b = back(mine, 2 * half)
    own_acts[0] = (b * slope[...]).astype(bf16)
    own_acts[1] = (b * gate[...]).astype(bf16)

    quarter = (width // 128 + STRIPS) // STRIPS * 128
    strips = [(at, min(at + quarter, width)) for at in range(0, width, quarter)]
    count = len(strips)

    def spans(begin, end):
        return [(at, min(STEP, end - at)) for at in range(begin, end, STEP)]

    def exchange(stage, i, src, dst, target):
        return pltpu.make_async_remote_copy(
            src_ref=src, dst_ref=dst, send_sem=rs_send.at[stage * count + i],
            recv_sem=rs_recv.at[stage * count + i], device_id=target, device_id_type=MESH,
        )

    def cols(i):
        begin, end = strips[i]
        return pl.ds(begin, end - begin)

    core = [exchange(0, i, send1.at[:, cols(i)], recv1.at[:, cols(i)], sib) for i in range(count)]
    second = [exchange(1, i, send2.at[:, cols(i)], recv2.at[:, cols(i)], x_nbr) for i in range(count)]
    third = [
        exchange(2, i, send3.at[pl.ds(0, (nz - 1) * tok), cols(i)], recv3.at[:, cols(i)], z_nbrs[0])
        for i in range(count)
    ]

    def first_stage(i):
        for at, size in spans(*strips[i]):
            span = slice(at, at + size)
            value = jnp.dot(own_acts[0], w[:, span], preferred_element_type=f32)
            value += jnp.dot(own_acts[1], wu[:, span], preferred_element_type=f32)
            send1[:, span] = value[side_rows:].astype(bf16)
            acc[:, span] = value[:side_rows]
        core[i].start()

    def second_stage(i):
        span = slice(*strips[i])
        core[i].wait()
        send2[:, span] = (acc[line:, span] + recv1[line:, span].astype(f32)).astype(bf16)
        second[i].start()
        acc[:line, span] = acc[:line, span] + recv1[:line, span].astype(f32)

    def third_stage(i):
        span = slice(*strips[i])
        second[i].wait()
        value = acc[:line, span] + recv2[:, span].astype(f32)
        send3[:, span] = value.astype(bf16)
        for k in range(1, nz):
            exchange(
                2, i, send3.at[rows(zs[k]), cols(i)], recv3.at[pl.ds((k - 1) * tok, tok), cols(i)], z_nbrs[k - 1]
            ).start()
        acc[:line, span] = value

    def last_stage(i):
        span = slice(*strips[i])
        third[i].wait()
        total = acc[rows(z), span]
        for k in range(1, nz):
            total = total + recv3[(k - 1) * tok : k * tok, span].astype(f32)
        gt_out[:, span] = total.astype(bf16)

    cuts = spans(0, width)
    middle = len(cuts) // 2

    def weight_term(k, right, part):
        if part == 0:
            turned[...] = acts[k].T
        for at, size in cuts[middle:] if part else cuts[:middle]:
            value = jnp.dot(turned[...], right[:, at : at + size], preferred_element_type=f32)
            gw[:, k * width + at : k * width + at + size] = value.astype(bf16)

    def keep_own():
        for k in range(2):
            acts[k, mine, :] = own_acts[k, :, :half]
        acts[2, mine, :] = (gate[:, :half] * up[:, :half] * scale_of(mine)).astype(bf16)

    def pass_rows():
        for d in range(1, nz):
            at_distance(d, cross_last)
        for zz in range(nz):
            arrived(0, 1, 1, zz)
            sib_send(0, 1, 1, zz)

    def pass_column(side, zz):
        arrived(1, 1, 0, zz)
        sib_send(1, 1, 0, zz)

    def pass_grads():
        for d in range(1, nz):
            at_distance(d, pass_column)
        for zz in range(nz):
            arrived(1, 1, 1, zz)
            sib_send(1, 1, 1, zz)

    def other_gate():
        sib_arrived(0, 1)
        gate[:, :half] = lax.dot_general(xs[other, :], w[:half, :width], contract, preferred_element_type=f32)

    def other_up():
        up[:, :half] = lax.dot_general(xs[other, :], wu[:half], contract, preferred_element_type=f32)
        derive(half)

    def other_back():
        sib_arrived(1, 1)
        b = back(other, half)
        acts[0, other, :] = (b * slope[:, :half]).astype(bf16)
        acts[1, other, :] = (b * gate[:, :half]).astype(bf16)
        acts[2, other, :] = (gate[:, :half] * up[:, :half] * scale_of(other)).astype(bf16)

    fill = [pass_rows, pass_grads, keep_own, other_gate, other_up, other_back]
    for k, right in enumerate((xs, xs, gs)):
        for part in range(2):
            fill.append(functools.partial(weight_term, k, right, part))

    for i in range(count):
        first_stage(i)
        if i > 0:
            second_stage(i - 1)
    second_stage(count - 1)
    done = 0
    for i in range(-1, count):
        if i >= 0:
            third_stage(i)
        upto = FILLS[i + 1] if i + 1 < count else len(fill)
        for act in fill[done:upto]:
            act()
        done = upto

    def sent(p, ry, side, chunks):
        s = slot(ry, 0, 0, 0)
        move(p, s, s, z_sides[side], sz.at[(p * 2 + ry) * 2 + side], landing(p, ry, 0, 0), chunks).wait_send()

    def to_y(p, chunks):
        move(p, 0, 0, y_nbr, sy.at[p], landing(p, 1, 0, 0), chunks).wait_send()

    for p in range(2):
        for ry in range(2):
            for side in range(2):
                if p == 1 and ry == 1:
                    pl.when(has_side[side])(lambda: sent(p, ry, side, 1))
                    continue
                for depth in range(nz - 1):
                    pl.when(side_depth[side] == depth)(lambda: sent(p, ry, side, depth + 1))
            move(p, 0, 0, sib, ss.at[p, ry], sib_recv.at[p, ry], 2 * nz).wait_send()
        move(p, 0, 0, x_nbr, sx.at[p], landing(p, 0, 1, 0), nz).wait_send()
        if p == 0:
            to_y(p, nz + 1)
        else:
            pl.when(at_end)(lambda: to_y(p, 2 * nz - 1))
            pl.when(jnp.logical_not(at_end))(lambda: to_y(p, 2 * nz - 2))
    for i in range(count):
        last_stage(i)


def store_kernel(gt, gw, gt_out, gw_out, sems):
    copies = [
        pltpu.make_async_copy(gt, gt_out, sems.at[0]),
        pltpu.make_async_copy(gw, gw_out.at[0], sems.at[1]),
    ]
    for copy in copies:
        copy.start()
    for copy in copies:
        copy.wait()


def dense_shards(tokens, grad_out, route_ids, route_prob, device_expert, unit_count, expert_weights):
    tok, width = tokens.shape
    devices = lax.axis_size("expert")
    nz = devices // 4
    experts = 5 * devices // 16
    half = expert_weights.shape[1] // lax.axis_size("dp")
    spare = 128 - width % 128
    assert 3 * experts <= spare
    padded = width + spare
    replica = devices * tok
    line = nz * tok
    top = route_ids.shape[1]
    bf16, f32 = jnp.bfloat16, jnp.float32
    vmem = pltpu.VMEM
    dma = pltpu.SemaphoreType.DMA
    any_spec = pl.BlockSpec(memory_space=pl.ANY)
    vmem_spec = pl.BlockSpec(memory_space=pltpu.VMEM)
    kept = 2 * (tok * padded + half * (-(-3 * width // 128) * 128))
    gt, gw = pl.pallas_call(
        functools.partial(split_kernel, nz, half, tok, width, experts),
        out_shape=(pltpu.VMEM((tok, width), bf16), pltpu.VMEM((half, 3 * width), bf16)),
        in_specs=[any_spec] * 7,
        out_specs=(vmem_spec, vmem_spec),
        scratch_shapes=[
            vmem((2 * replica, width), bf16), vmem((2 * replica, padded), bf16), vmem((tok, width), bf16),
            vmem((top, tok), jnp.int32), vmem((top, tok), f32),
            pltpu.SMEM((devices,), jnp.int32), pltpu.SMEM((devices,), jnp.int32),
            vmem((2 * half, 3 * width), bf16), vmem((2 * half, width), bf16),
            vmem((replica, 2 * half), f32), vmem((replica, 2 * half), f32), vmem((replica, 2 * half), f32),
            vmem((2, replica, 2 * half), bf16), vmem((3, 2 * replica, half), bf16), vmem((half, 2 * replica), bf16),
            vmem((2 * line, width), f32),
            vmem((2 * line, width), bf16), vmem((2 * line, width), bf16),
            vmem((line, width), bf16), vmem((line, width), bf16),
            vmem((line, width), bf16), vmem(((nz - 1) * tok, width), bf16),
            dma((8,)), dma((2, 4 * nz)), dma((2, 2)), dma((8,)), dma((2,)), dma((2,)), dma((2, 2)),
            dma((3 * STRIPS,)), dma((3 * STRIPS,)),
        ],
        compiler_params=pltpu.CompilerParams(
            collective_id=0, has_side_effects=True, vmem_limit_bytes=VMEM_BYTES - kept
        ),
        name="split_backward",
    )(tokens, grad_out, expert_weights, route_ids.T, route_prob.T, device_expert, unit_count)
    return pl.pallas_call(
        store_kernel,
        out_shape=(
            jax.ShapeDtypeStruct((tok, width), bf16),
            jax.ShapeDtypeStruct((1, half, 3 * width), bf16),
        ),
        in_specs=[vmem_spec] * 2,
        out_specs=[any_spec] * 2,
        scratch_shapes=[dma((2,))],
        compiler_params=pltpu.CompilerParams(vmem_limit_bytes=1024 * 1024),
        name="store_outputs",
    )(gt, gw)


def shards(tokens, grad_out, route_ids, *rest):
    token_count = tokens.shape[0]
    capacity = token_count * route_ids.shape[1] * 4 // lax.axis_size("expert")
    form = dense_shards if capacity >= token_count else routed_shards
    return form(tokens, grad_out, route_ids, *rest)


def solution(mesh):
    in_specs = (P(AXES, None),) * 4 + (P(), P(), P("expert", None, None))
    out_specs = (P(AXES, None), P("expert", "dp", None))
    return jax.shard_map(shards, mesh=mesh, in_specs=in_specs, out_specs=out_specs, check_vma=False)
```
